128 devices in a mesh: tok: 16 (over z, x_hi, core), req: 8 (over x_lo, y).
Axes of the slice: x: 4 (x_hi: 2, x_lo: 2; x = x_hi * 2 + x_lo), y: 4, z: 4, core: 2. Of those that a mesh axis runs over, the one named last changes fastest.
Arguments:
- query_rows: bfloat16 [8, 4096, 7168], P('req', 'tok'), may hold values from -16 to 16
- key_rows: bfloat16 [8, 4096, 7168], P('req', 'tok'), may hold values from -16 to 16
- value_rows: bfloat16 [8, 4096, 7168], P('req', 'tok'), may hold values from -6 to 6
- lengths: int32 [8, 6], P('req'), may hold values from 1 to 2048, 4096 in all within a row
- cache_blocks: bfloat16 [8, 128, 2, 32, 3584], P('req', 'tok'), may hold values from -6 to 6
- destinations: int32 [8, 128, 1], P('req', 'tok'), may hold values from 0 to 7; in each aligned block of 8 rows (0 to 7, 8 to 15, ..., all dimensions but the last counted through in order) at most 2 rows name the same one
Outputs:
- attended: bfloat16 [8, 4096, 7168], P('req', 'tok')
- moved_cache: bfloat16 [8, 8, 2, 2, 16, 32, 3584], P('req', None, None, None, None, 'tok')
The draws below stay inside these ranges and needn't reach their ends.
Inputs may be any that keep to these rules, and one draw needn't show every extreme that they name: The 6 lengths of each span sum to 4096, and the longest of every span is exactly 2048. `destinations`: of the 8 rows of one device (aligned blocks of 8 rows), at most 2 name the same group, and in every draw some device names one group exactly 2 times.
All inputs are finite; a program needn't handle non-finite values.
Results may differ from the reference program's by a relative error of at most 0.0037.
Values may be sent and summed in bfloat16 or wider, within the bound.
A program may use at most 192 MiB of HBM per device.

```python
import math
import jax
import jax.numpy as jnp
import numpy as np
from jax import lax

H = 32
HD = 224
NSEQ = 6
BPD = 8
CAP = 2
SPAN = 4096
SPANS = 8
LONGEST = 2048
BH = 3584
N_TOK = 16
N_REQ = 8


def drawn_pair(key):
    base = jax.random.fold_in(key, 4711)
    key_query, key_keys = jax.random.split(base, 2)
    shape = (SPANS, SPAN, H, HD)
    query_draw = jnp.clip(jax.random.normal(key_query, shape, jnp.float32), -6.0, 6.0)
    key_draw = jnp.clip(jax.random.normal(key_keys, shape, jnp.float32), -6.0, 6.0)
    query_draw = jnp.clip(query_draw, -16.0, 16.0).reshape(SPANS, SPAN, H * HD)
    key_draw = jnp.clip(key_draw, -16.0, 16.0).reshape(SPANS, SPAN, H * HD)
    return (query_draw, key_draw)


def draw_query_rows(key, part):
    return drawn_pair(key)[0].astype(jnp.bfloat16)


def draw_key_rows(key, part):
    return drawn_pair(key)[1].astype(jnp.bfloat16)


def block_levels(key, extent, pieces, least, largest):
    loudness = 1.0
    for position, blocks in pieces:
        heights = jax.random.uniform(jax.random.fold_in(jax.random.fold_in(key, 6), position), (blocks,), jnp.float32, least / len(pieces), largest / len(pieces))
        loudness = loudness * jnp.repeat(jnp.exp(heights), extent[position] // blocks).reshape((-1,) + (1,) * (len(extent) - 1 - position))
    return loudness


def profile(amount, total, limit, skew):
    loads = [(1 << 20) // math.isqrt(standing ** skew) + 1 for standing in range(2, amount + 1)]
    spare, counts = total - limit - (amount - 1), [1] * (amount - 1)
    while spare > 0:
        candidates = [i for i in range(amount - 1) if counts[i] < limit]
        whole, left = sum([loads[i] for i in candidates]), spare
        for i in candidates:
            extra = min(limit - counts[i], max(1, left * loads[i] // whole), spare)
            counts[i] = counts[i] + extra
            spare = spare - extra
    return np.array([limit] + counts)


def ragged(stream_key, number_of, total, bound, slope):
    if number_of == 2:
        one = jax.random.randint(stream_key, (), max(1, total - bound), min(bound, total - 1) + 1)
        return jnp.stack([one, total - one])
    sizes = jnp.asarray(profile(number_of, total, bound, slope), jnp.int32)
    twos = (number_of - 1) // 2
    donor, receiver = sizes[1:1 + 2 * twos:2], sizes[2:2 + 2 * twos:2]
    slack = jnp.minimum(donor - 1, bound - receiver)
    passed = jax.random.randint(jax.random.fold_in(stream_key, 1), (twos,), 0, 1 << 20) % (slack + 1)
    sizes = sizes.at[1:1 + 2 * twos:2].set(donor - passed).at[2:2 + 2 * twos:2].set(receiver + passed)
    return sizes[jax.random.permutation(jax.random.fold_in(stream_key, 2), number_of)]


def routed_block(rng, own, number, rows, amount, top, most, lean):
    order = jax.random.permutation(rng, amount)
    heavy_load, usual = portions_of(amount, rows * top, most, lean, True), portions_of(amount, rows * top, most, lean, False)
    places = jnp.arange(amount)

    def named(sizes, rotation):
        used = int((sizes > 0).sum())
        fixed = max(1, used // 4)
        shifted = fixed + (places - fixed + rotation * (used - fixed)) % max(1, amount - fixed)
        return jnp.zeros((amount,), jnp.int32).at[order[jnp.where(places < fixed, places, shifted)]].set(jnp.asarray(sizes, jnp.int32))

    sizes = jnp.where(number % 4 == 0, named(heavy_load, number // 4), named(usual, number - number // 4 - 1))
    mixed = jax.random.permutation(jax.random.fold_in(own, 3), amount)
    giver, taker = mixed[0:amount // 2 * 2:2], mixed[1:amount // 2 * 2:2]
    room = jnp.minimum(sizes[giver] - 1, most - sizes[taker]) // 2
    room = jnp.where((giver == order[0]) | (taker == order[0]) | (sizes[taker] == 0), 0, jnp.maximum(room, 0))
    shifted = jax.random.randint(jax.random.fold_in(own, 4), (amount // 2,), 0, 1 << 20) % (room + 1)
    sizes = sizes.at[giver].add(-shifted).at[taker].add(shifted)
    items = jnp.searchsorted(jnp.cumsum(sizes), jnp.arange(rows * top), side="right").astype(jnp.int32)
    table = items.reshape(top, rows).T
    table = table[jax.random.permutation(jax.random.fold_in(own, 1), rows)]
    rotation = jax.random.randint(jax.random.fold_in(own, 2), (rows, 1), 0, top)
    return jnp.take_along_axis(table, (jnp.arange(top)[None, :] + rotation) % top, axis=1)


def portions_of(count, total, most, lean, full):
    loads = [(1 << 20) // math.isqrt(grade ** lean) + 1 for grade in range(1, count + 1)]
    largest = most if full else min(most, max(-(-total // count), total * loads[0] // sum(loads)))
    least = 1 if total - largest >= count - 1 else 0
    counts, surplus = [largest] + [least] * (count - 1), total - largest - least * (count - 1)
    while surplus > 0:
        candidates = [i for i in range(1, count) if counts[i] < largest] or [i for i in range(1, count) if counts[i] < most]
        pool, remaining = sum([loads[i] for i in candidates]), surplus
        for i in candidates:
            more = min(most - counts[i], max(1, remaining * loads[i] // pool), surplus)
            counts[i] = counts[i] + more
            surplus = surplus - more
    return np.array(counts)


def centred(rng, dims, width, bound, cuts=(), held_as=jnp.bfloat16):
    array = jax.random.normal(rng, dims, jnp.float32) * width
    if len(cuts) > 0:
        array = block_levels(rng, dims, cuts, -0.22, 0.18) * array
    return jnp.clip(array, min=-bound, max=bound).astype(held_as)


def setup_inputs(seed: int = 0) -> dict:
    seeds = jax.random.split(jax.random.key(seed), 7)
    query_rows = draw_query_rows(jax.random.fold_in(seeds[6], 71), 0)
    key_rows = draw_key_rows(jax.random.fold_in(seeds[6], 71), 0)
    value_rows = centred(seeds[2], (SPANS, SPAN, H * HD), 1.0, 6.0, ((0, 8), (1, 16)))
    lengths = jax.vmap(lambda own: ragged(own, NSEQ, SPAN, LONGEST, 2))(jax.random.split(seeds[3], SPANS)).reshape((SPANS, NSEQ)).astype(jnp.int32)
    cache_blocks = centred(seeds[4], (N_REQ, N_TOK * BPD, 2, H, BH), 1.0, 6.0, ((0, 8), (1, 16)))
    destinations_keys = jax.random.split(jax.random.fold_in(seeds[5], 1), N_REQ * (N_TOK * BPD) // BPD)
    destinations_turns = jax.random.permutation(jax.random.fold_in(seeds[5], 3), N_REQ * (N_TOK * BPD) // BPD)
    destinations = jax.vmap(lambda own, number: routed_block(jax.random.fold_in(seeds[5], 2), own, number, BPD, N_REQ, 1, CAP, 2))(destinations_keys, destinations_turns).reshape((N_REQ, N_TOK * BPD, 1))
    return {"query_rows": query_rows, "key_rows": key_rows, "value_rows": value_rows, "lengths": lengths, "cache_blocks": cache_blocks, "destinations": destinations}


def segment_ids(lengths):
    ends = jnp.cumsum(lengths, axis=-1)
    positions = jnp.arange(SPAN, dtype=jnp.int32)
    return jnp.sum((positions[None, :, None] >= ends[:, None, :]).astype(jnp.int32), axis=-1)


def head_attend(query_head, key_head, value_head, segments):
    positions = jnp.arange(query_head.shape[0], dtype=jnp.int32)
    scores = jnp.dot(query_head, key_head.T, preferred_element_type=jnp.float32) * (query_head.shape[1] ** -0.5)
    visible = (segments[:, None] == segments[None, :]) & (positions[:, None] >= positions[None, :])
    scores = jnp.where(visible, scores, -1e30)
    row_max = jnp.max(scores, axis=1, keepdims=True)
    weights = jnp.where(visible, jnp.exp(scores - row_max), 0.0)
    row_total = jnp.sum(weights, axis=1, keepdims=True)
    summed = jnp.dot(weights.astype(jnp.bfloat16), value_head, preferred_element_type=jnp.float32)
    return (summed / row_total).astype(jnp.bfloat16)


def relocate(cache_blocks, destinations):
    targets = destinations[..., 0].reshape(N_REQ, N_TOK, BPD)
    positions = jnp.arange(BPD, dtype=jnp.int32)
    earlier = (targets[..., :, None] == targets[..., None, :]) & (positions[None, :] < positions[:, None])
    slot_rank = jnp.sum(earlier.astype(jnp.int32), axis=-1)
    target_swap = jnp.transpose(targets, (1, 0, 2))
    rank_swap = jnp.transpose(slot_rank, (1, 0, 2))
    groups = jnp.arange(N_REQ, dtype=jnp.int32)
    slots = jnp.arange(CAP, dtype=jnp.int32)
    match = (target_swap[None, :, :, None, :] == groups[:, None, None, None, None]) & (rank_swap[None, :, :, None, :] == slots[None, None, None, :, None])
    which = jnp.sum(jnp.where(match, positions, 0), axis=-1).astype(jnp.int32)
    valid = jnp.any(match, axis=-1)
    row_index = jnp.arange(N_TOK, dtype=jnp.int32)[None, :, None, None] * BPD + which
    source_index = jnp.arange(N_REQ, dtype=jnp.int32)[None, None, :, None] + 0 * row_index
    picked = cache_blocks[source_index, row_index]
    placed = jnp.where(valid[..., None, None, None], picked, jnp.zeros((), cache_blocks.dtype))
    return jnp.transpose(placed, (0, 2, 3, 4, 1, 5, 6))


def reference(query_rows, key_rows, value_rows, lengths, cache_blocks, destinations):
    segments = segment_ids(lengths)

    def to_heads(rows_in):
        return jnp.transpose(rows_in.reshape(SPANS, SPAN, H, HD), (0, 2, 1, 3))

    def one_span(item):
        query_span, key_span, value_span, span_segments = item

        def one_head(parts):
            return head_attend(parts[0], parts[1], parts[2], span_segments)

        return lax.map(one_head, (query_span, key_span, value_span))

    heads = lax.map(one_span, (to_heads(query_rows), to_heads(key_rows), to_heads(value_rows), segments))
    attended = jnp.transpose(heads, (0, 2, 1, 3)).reshape(SPANS, SPAN, H * HD)
    moved_cache = relocate(cache_blocks, destinations)
    return (attended, moved_cache)
```

```python
import functools

import jax
import jax.numpy as jnp
from jax import lax
from jax.experimental import pallas as pl
from jax.experimental.pallas import tpu as pltpu
from jax.sharding import PartitionSpec as P

HD = 224
CAP = 2
BLOCK = 512
NEG = -1e30


def segment_ids(lengths_row, span_length):
    ends = jnp.cumsum(lengths_row)
    positions = jnp.arange(span_length, dtype=jnp.int32)
    return jnp.sum((positions[:, None] >= ends[None, :]).astype(jnp.int32), axis=1)


def attention_kernel(first_block_ref, q_ref, k_ref, v_ref, qseg_ref, kseg_ref, o_ref, m_ref, l_ref, acc_ref):
    qi = pl.program_id(0)
    rows, width = q_ref.shape
    heads_here = width // HD
    columns = lax.broadcasted_iota(jnp.int32, (1, width), 1)
    head_masks = [(columns >= h * HD) & (columns < (h + 1) * HD) for h in range(heads_here)]
    q = q_ref[...]
    zero = jnp.zeros((), q.dtype)
    queries = [jnp.where(mask, q, zero) for mask in head_masks]
    query_seg = qseg_ref[...]
    query_pos = qi * rows + lax.broadcasted_iota(jnp.int32, (rows, 1), 0)
    m_ref[...] = jnp.full(m_ref.shape, NEG, jnp.float32)
    l_ref[...] = jnp.zeros(l_ref.shape, jnp.float32)
    acc_ref[...] = jnp.zeros(acc_ref.shape, jnp.float32)
    scale = HD ** (-0.5)

    def body(kb, carry):
        start = pl.multiple_of(kb * rows, rows)
        keys = k_ref[pl.ds(start, rows), :]
        values = v_ref[pl.ds(start, rows), :]
        key_seg = kseg_ref[:, pl.ds(start, rows)]
        key_pos = start + lax.broadcasted_iota(jnp.int32, (1, rows), 1)
        visible = (query_seg == key_seg) & (query_pos >= key_pos)
        alpha_cols = jnp.zeros((rows, width), jnp.float32)
        update = jnp.zeros((rows, width), jnp.float32)
        for h in range(heads_here):
            scores = lax.dot_general(
                queries[h], keys, (((1,), (1,)), ((), ())), preferred_element_type=jnp.float32
            ) * scale
            scores = jnp.where(visible, scores, NEG)
            m_old = m_ref[h]
            m_new = jnp.maximum(m_old, jnp.max(scores, axis=1, keepdims=True))
            alpha = jnp.exp(m_old - m_new)
            weights = jnp.where(visible, jnp.exp(scores - m_new), 0.0)
            l_ref[h] = alpha * l_ref[h] + jnp.sum(weights, axis=1, keepdims=True)
            m_ref[h] = m_new
            masked_values = jnp.where(head_masks[h], values, zero)
            update = update + jnp.dot(
                weights.astype(jnp.bfloat16), masked_values, preferred_element_type=jnp.float32
            )
            alpha_cols = jnp.where(head_masks[h], alpha, alpha_cols)
        acc_ref[...] = alpha_cols * acc_ref[...] + update
        return carry

    lax.fori_loop(first_block_ref[qi], qi + 1, body, 0)
    totals = jnp.ones((rows, width), jnp.float32)
    for h in range(heads_here):
        totals = jnp.where(head_masks[h], l_ref[h], totals)
    o_ref[...] = (acc_ref[...] / totals).astype(o_ref.dtype)


def attend_local(query, key, value, segments):
    length, width = query.shape
    heads_here = width // HD
    blocks = length // BLOCK
    ends = jnp.cumsum(jnp.bincount(segments, length=8))
    starts = ends - jnp.bincount(segments, length=8)
    first_query = segments[::BLOCK]
    first_block = (starts[first_query] // BLOCK).astype(jnp.int32)
    qseg = segments.reshape(length, 1)
    kseg = segments.reshape(1, length)
    visible_pairs = length * length // 2
    cost = pl.CostEstimate(
        flops=int(8 * visible_pairs * width),
        transcendentals=int(heads_here * visible_pairs),
        bytes_accessed=int(4 * length * width * 2),
    )
    return pl.pallas_call(
        attention_kernel,
        out_shape=jax.ShapeDtypeStruct((length, width), query.dtype),
        grid_spec=pltpu.PrefetchScalarGridSpec(
            num_scalar_prefetch=1,
            grid=(blocks,),
            in_specs=[
                pl.BlockSpec((BLOCK, width), lambda i, fb: (i, 0)),
                pl.BlockSpec((length, width), lambda i, fb: (0, 0), pipeline_mode=pl.Buffered(1)),
                pl.BlockSpec((length, width), lambda i, fb: (0, 0), pipeline_mode=pl.Buffered(1)),
                pl.BlockSpec((BLOCK, 1), lambda i, fb: (i, 0)),
                pl.BlockSpec((1, length), lambda i, fb: (0, 0)),
            ],
            out_specs=pl.BlockSpec((BLOCK, width), lambda i, fb: (i, 0)),
            scratch_shapes=[
                pltpu.VMEM((heads_here, BLOCK, 1), jnp.float32),
                pltpu.VMEM((heads_here, BLOCK, 1), jnp.float32),
                pltpu.VMEM((BLOCK, width), jnp.float32),
            ],
        ),
        compiler_params=pltpu.CompilerParams(dimension_semantics=("arbitrary",)),
        cost_estimate=cost,
    )(first_block, query, key, value, qseg, kseg)


def regroup_attend(query_rows, key_rows, value_rows, segments):
    tok_count = lax.axis_size("tok")
    token_rows = query_rows.shape[1]
    feature_width = query_rows.shape[2]
    group_width = feature_width // tok_count

    def to_heads(rows_in):
        split = rows_in[0].reshape(token_rows, tok_count, group_width)
        gathered = lax.all_to_all(split, "tok", split_axis=1, concat_axis=0, tiled=True)
        return gathered.reshape(token_rows * tok_count, group_width)

    attended = attend_local(to_heads(query_rows), to_heads(key_rows), to_heads(value_rows), segments)
    by_source = attended.reshape(tok_count, token_rows, group_width).transpose(1, 0, 2)
    returned = lax.all_to_all(by_source, "tok", split_axis=1, concat_axis=1, tiled=True)
    return returned.reshape(1, token_rows, feature_width)


def relocate(cache_blocks, destinations):
    groups = lax.axis_size("req")
    tok_count = lax.axis_size("tok")
    local_blocks = cache_blocks[0]
    block_count, kv_count, heads_all, entries = local_blocks.shape
    split = local_blocks.reshape(block_count, kv_count, tok_count, heads_all // tok_count, entries)
    by_head = lax.all_to_all(split, "tok", split_axis=2, concat_axis=2, tiled=True)
    targets = lax.all_gather(destinations[0, :, 0], "tok")
    positions = jnp.arange(block_count, dtype=jnp.int32)
    earlier = (targets[:, :, None] == targets[:, None, :]) & (positions[None, None, :] < positions[None, :, None])
    slot_rank = jnp.sum(earlier.astype(jnp.int32), axis=2)
    group_ids = jnp.arange(groups, dtype=jnp.int32)
    slot_ids = jnp.arange(CAP, dtype=jnp.int32)
    placing = (
        (targets[:, :, None, None] == group_ids[None, None, :, None])
        & (slot_rank[:, :, None, None] == slot_ids[None, None, None, :])
    ).astype(cache_blocks.dtype)
    outgoing = jnp.einsum(
        "tbgc,bktjy->gcktjy", placing, by_head, preferred_element_type=jnp.float32
    ).astype(cache_blocks.dtype)
    arrived = lax.all_to_all(outgoing, "req", split_axis=0, concat_axis=0, tiled=True)
    return arrived[None]


def on_device(query_rows, key_rows, value_rows, lengths, cache_blocks, destinations):
    span_length = query_rows.shape[1] * lax.axis_size("tok")
    segments = segment_ids(lengths[0], span_length)
    attended = regroup_attend(query_rows, key_rows, value_rows, segments)
    moved_cache = relocate(cache_blocks, destinations)
    return (attended, moved_cache)


def solution(mesh):
    return jax.shard_map(
        on_device,
        mesh=mesh,
        in_specs=(
            P("req", "tok", None),
            P("req", "tok", None),
            P("req", "tok", None),
            P("req", None),
            P("req", "tok", None, None, None),
            P("req", "tok", None),
        ),
        out_specs=(P("req", "tok", None), P("req", None, None, None, None, "tok", None)),
        check_vma=False,
    )
```

```python
import functools

import jax
import jax.numpy as jnp
from jax import lax
from jax.experimental import pallas as pl
from jax.experimental.pallas import tpu as pltpu
from jax.sharding import PartitionSpec as P

HD = 224
CAP = 2
NEG = -1e30


def segment_ids(lengths_row, span_length):
    ends = jnp.cumsum(lengths_row)
    positions = jnp.arange(span_length, dtype=jnp.int32)
    return jnp.sum((positions[:, None] >= ends[None, :]).astype(jnp.int32), axis=1)


def attention_kernel(first_ref, seg_first_ref, seg_last_ref, q_ref, k_ref, v_ref, qseg_ref, kseg_ref, o_ref,
                     m_ref, l_ref, acc_ref, q_sc):
    qi = pl.program_id(0)
    width, rows = q_ref.shape[1], q_ref.shape[2]
    heads_here = width // HD
    eye_rows = lax.broadcasted_iota(jnp.int32, (rows, rows), 0) == lax.broadcasted_iota(jnp.int32, (rows, rows), 1)
    eye = eye_rows.astype(jnp.bfloat16)
    nt = (((1,), (1,)), ((), ()))
    for h in range(heads_here):
        q_sc[h] = lax.dot_general(
            eye, q_ref[0, h * HD:(h + 1) * HD, :], nt, preferred_element_type=jnp.float32
        ).astype(jnp.bfloat16)
    m_ref[...] = jnp.full(m_ref.shape, NEG, jnp.float32)
    l_ref[...] = jnp.zeros(l_ref.shape, jnp.float32)
    acc_ref[...] = jnp.zeros(acc_ref.shape, jnp.float32)
    scale = HD ** (-0.5)
    query_seg = qseg_ref[...]
    query_pos = qi * rows + lax.broadcasted_iota(jnp.int32, (rows, 1), 0)

    def step(kb, masked):
        if masked:
            key_seg = kseg_ref[kb]
            key_pos = kb * rows + lax.broadcasted_iota(jnp.int32, (1, rows), 1)
            visible = (query_seg == key_seg) & (query_pos >= key_pos)
        for h in range(heads_here):
            keys = k_ref[kb, h * HD:(h + 1) * HD, :]
            scores = jnp.dot(q_sc[h], keys, preferred_element_type=jnp.float32) * scale
            if masked:
                scores = jnp.where(visible, scores, NEG)
            m_old = m_ref[h]
            m_new = jnp.maximum(m_old, jnp.max(scores, axis=1, keepdims=True))
            alpha = jnp.exp(m_old - m_new)
            weights = jnp.exp(scores - m_new)
            if masked:
                weights = jnp.where(visible, weights, 0.0)
            l_ref[h] = alpha * l_ref[h] + jnp.sum(weights, axis=1, keepdims=True)
            m_ref[h] = m_new
            values = v_ref[kb, h * HD:(h + 1) * HD, :]
            acc_ref[h] = alpha * acc_ref[h] + lax.dot_general(
                weights.astype(jnp.bfloat16), values, nt, preferred_element_type=jnp.float32
            )

    def body(kb, carry):
        full = (kb < qi) & (seg_first_ref[kb] == seg_last_ref[qi])

        @pl.when(full)
        def _():
            step(kb, False)

        @pl.when(jnp.logical_not(full))
        def _():
            step(kb, True)

        return carry

    lax.fori_loop(first_ref[qi], qi + 1, body, 0)
    eye_out = (lax.broadcasted_iota(jnp.int32, (HD, HD), 0) == lax.broadcasted_iota(jnp.int32, (HD, HD), 1)).astype(jnp.bfloat16)
    for h in range(heads_here):
        out_rows = (acc_ref[h] / l_ref[h]).astype(jnp.bfloat16)
        o_ref[0, h * HD:(h + 1) * HD, :] = lax.dot_general(
            eye_out, out_rows, nt, preferred_element_type=jnp.float32
        ).astype(o_ref.dtype)


def attend_local(query_t, key_t, value_t, lengths_row, segments):
    chunks, width, rows = query_t.shape
    heads_here = width // HD
    length = chunks * rows
    ends = jnp.cumsum(lengths_row)
    starts = ends - lengths_row
    seg_first = segments[::rows]
    seg_last = segments[rows - 1::rows]
    first_start = jnp.sum(
        jnp.where(seg_first[:, None] == jnp.arange(lengths_row.shape[0])[None, :], starts[None, :], 0), axis=1
    )
    first_chunk = (first_start // rows).astype(jnp.int32)
    qseg = segments.reshape(length, 1)
    kseg = segments.reshape(chunks, 1, rows)
    visible_pairs = length * length // 2
    cost = pl.CostEstimate(
        flops=int(4 * visible_pairs * width),
        transcendentals=int(heads_here * visible_pairs),
        bytes_accessed=int(4 * length * width * 2),
    )
    return pl.pallas_call(
        attention_kernel,
        out_shape=jax.ShapeDtypeStruct(query_t.shape, query_t.dtype),
        grid_spec=pltpu.PrefetchScalarGridSpec(
            num_scalar_prefetch=3,
            grid=(chunks,),
            in_specs=[
                pl.BlockSpec((1, width, rows), lambda i, *_: (i, 0, 0)),
                pl.BlockSpec((chunks, width, rows), lambda i, *_: (0, 0, 0), pipeline_mode=pl.Buffered(1)),
                pl.BlockSpec((chunks, width, rows), lambda i, *_: (0, 0, 0), pipeline_mode=pl.Buffered(1)),
                pl.BlockSpec((rows, 1), lambda i, *_: (i, 0)),
                pl.BlockSpec((chunks, 1, rows), lambda i, *_: (0, 0, 0)),
            ],
            out_specs=pl.BlockSpec((1, width, rows), lambda i, *_: (i, 0, 0)),
            scratch_shapes=[
                pltpu.VMEM((heads_here, rows, 1), jnp.float32),
                pltpu.VMEM((heads_here, rows, 1), jnp.float32),
                pltpu.VMEM((heads_here, rows, HD), jnp.float32),
                pltpu.VMEM((heads_here, rows, HD), jnp.bfloat16),
            ],
        ),
        compiler_params=pltpu.CompilerParams(dimension_semantics=("arbitrary",)),
        cost_estimate=cost,
    )(first_chunk, seg_first, seg_last, query_t, key_t, value_t, qseg, kseg)


def regroup_attend(query_rows, key_rows, value_rows, lengths_row, segments):
    tok_count = lax.axis_size("tok")
    token_rows = query_rows.shape[1]
    feature_width = query_rows.shape[2]
    group_width = feature_width // tok_count

    def to_heads(rows_in):
        split = rows_in[0].reshape(token_rows, tok_count, group_width)
        gathered = lax.all_to_all(split, "tok", split_axis=1, concat_axis=1, tiled=True)
        return gathered.transpose(1, 2, 0)

    attended_t = attend_local(
        to_heads(query_rows), to_heads(key_rows), to_heads(value_rows), lengths_row, segments
    )
    by_source = attended_t.transpose(2, 0, 1)
    returned = lax.all_to_all(by_source, "tok", split_axis=1, concat_axis=1, tiled=True)
    return returned.reshape(1, token_rows, feature_width)


def relocate(cache_blocks, targets):
    groups = lax.axis_size("req")
    tok_count = lax.axis_size("tok")
    local_blocks = cache_blocks[0]
    block_count, kv_count, heads_all, entries = local_blocks.shape
    split = local_blocks.reshape(block_count, kv_count, tok_count, heads_all // tok_count, entries)
    by_head = lax.all_to_all(split, "tok", split_axis=2, concat_axis=2, tiled=True)
    positions = jnp.arange(block_count, dtype=jnp.int32)
    earlier = (targets[:, :, None] == targets[:, None, :]) & (positions[None, None, :] < positions[None, :, None])
    slot_rank = jnp.sum(earlier.astype(jnp.int32), axis=2)
    group_ids = jnp.arange(groups, dtype=jnp.int32)
    slot_ids = jnp.arange(CAP, dtype=jnp.int32)
    placing = (
        (targets[:, :, None, None] == group_ids[None, None, :, None])
        & (slot_rank[:, :, None, None] == slot_ids[None, None, None, :])
    ).astype(cache_blocks.dtype)
    outgoing = jnp.einsum(
        "tbgc,bktjy->gcktjy", placing, by_head, preferred_element_type=jnp.float32
    ).astype(cache_blocks.dtype)
    arrived = lax.all_to_all(outgoing, "req", split_axis=0, concat_axis=0, tiled=True)
    return arrived[None]


def on_device(query_rows, key_rows, value_rows, lengths, cache_blocks, destinations):
    span_length = query_rows.shape[1] * lax.axis_size("tok")
    segments = segment_ids(lengths[0], span_length)
    targets = lax.all_gather(destinations[0, :, 0], "tok")
    targets, query_rows, key_rows, value_rows, cache_blocks = lax.optimization_barrier(
        (targets, query_rows, key_rows, value_rows, cache_blocks)
    )
    attended = regroup_attend(query_rows, key_rows, value_rows, lengths[0], segments)
    moved_cache = relocate(cache_blocks, targets)
    return (attended, moved_cache)


def solution(mesh):
    return jax.shard_map(
        on_device,
        mesh=mesh,
        in_specs=(
            P("req", "tok", None),
            P("req", "tok", None),
            P("req", "tok", None),
            P("req", None),
            P("req", "tok", None, None, None),
            P("req", "tok", None),
        ),
        out_specs=(P("req", "tok", None), P("req", None, None, None, None, "tok", None)),
        check_vma=False,
    )
```

```python
import functools

import jax
import jax.numpy as jnp
from jax import lax
from jax.experimental import pallas as pl
from jax.experimental.pallas import tpu as pltpu
from jax.sharding import PartitionSpec as P

HD = 224
CAP = 2
NEG = -1e30


def segment_ids(lengths_row, span_length):
    ends = jnp.cumsum(lengths_row)
    positions = jnp.arange(span_length, dtype=jnp.int32)
    return jnp.sum((positions[:, None] >= ends[None, :]).astype(jnp.int32), axis=1)


def attention_kernel(first_ref, seg_first_ref, seg_last_ref, q_ref, k_ref, v_ref, qseg_ref, kseg_ref, o_ref,
                     m_ref, l_ref, acc_ref, q_sc):
    qi = pl.program_id(0)
    width, rows = q_ref.shape[1], q_ref.shape[2]
    heads_here = width // HD
    eye_rows = lax.broadcasted_iota(jnp.int32, (rows, rows), 0) == lax.broadcasted_iota(jnp.int32, (rows, rows), 1)
    eye = eye_rows.astype(jnp.bfloat16)
    nt = (((1,), (1,)), ((), ()))
    for h in range(heads_here):
        q_sc[h] = lax.dot_general(
            eye, q_ref[0, h * HD:(h + 1) * HD, :], nt, preferred_element_type=jnp.float32
        ).astype(jnp.bfloat16)
    m_ref[...] = jnp.full(m_ref.shape, NEG, jnp.float32)
    l_ref[...] = jnp.zeros(l_ref.shape, jnp.float32)
    acc_ref[...] = jnp.zeros(acc_ref.shape, jnp.float32)
    scale = HD ** (-0.5)
    query_seg = qseg_ref[...]
    query_pos = qi * rows + lax.broadcasted_iota(jnp.int32, (rows, 1), 0)

    def step(kb, masked):
        if masked:
            key_seg = kseg_ref[kb]
            key_pos = kb * rows + lax.broadcasted_iota(jnp.int32, (1, rows), 1)
            visible = (query_seg == key_seg) & (query_pos >= key_pos)
        for h in range(heads_here):
            keys = k_ref[kb, h * HD:(h + 1) * HD, :]
            scores = jnp.dot(q_sc[h], keys, preferred_element_type=jnp.float32) * scale
            if masked:
                scores = jnp.where(visible, scores, NEG)
            m_old = m_ref[h]
            m_new = jnp.maximum(m_old, jnp.max(scores, axis=1, keepdims=True))
            alpha = jnp.exp(m_old - m_new)
            weights = jnp.exp(scores - m_new)
            if masked:
                weights = jnp.where(visible, weights, 0.0)
            l_ref[h] = alpha * l_ref[h] + jnp.sum(weights, axis=1, keepdims=True)
            m_ref[h] = m_new
            values = v_ref[kb, h * HD:(h + 1) * HD, :]
            acc_ref[h] = alpha * acc_ref[h] + lax.dot_general(
                weights.astype(jnp.bfloat16), values, nt, preferred_element_type=jnp.float32
            )

    def body(kb, carry):
        full = (kb < qi) & (seg_first_ref[kb] == seg_last_ref[qi])

        @pl.when(full)
        def _():
            step(kb, False)

        @pl.when(jnp.logical_not(full))
        def _():
            step(kb, True)

        return carry

    lax.fori_loop(first_ref[qi], qi + 1, body, 0)
    eye_out = (lax.broadcasted_iota(jnp.int32, (HD, HD), 0) == lax.broadcasted_iota(jnp.int32, (HD, HD), 1)).astype(jnp.bfloat16)
    for h in range(heads_here):
        out_rows = (acc_ref[h] / l_ref[h]).astype(jnp.bfloat16)
        o_ref[0, h * HD:(h + 1) * HD, :] = lax.dot_general(
            eye_out, out_rows, nt, preferred_element_type=jnp.float32
        ).astype(o_ref.dtype)


def attend_local(query_t, key_t, value_t, lengths_row, segments):
    chunks, width, rows = query_t.shape
    heads_here = width // HD
    length = chunks * rows
    ends = jnp.cumsum(lengths_row)
    starts = ends - lengths_row
    seg_first = segments[::rows]
    seg_last = segments[rows - 1::rows]
    first_start = jnp.sum(
        jnp.where(seg_first[:, None] == jnp.arange(lengths_row.shape[0])[None, :], starts[None, :], 0), axis=1
    )
    first_chunk = (first_start // rows).astype(jnp.int32)
    qseg = segments.reshape(length, 1)
    kseg = segments.reshape(chunks, 1, rows)
    visible_pairs = length * length // 2
    cost = pl.CostEstimate(
        flops=int(4 * visible_pairs * width),
        transcendentals=int(heads_here * visible_pairs),
        bytes_accessed=int(4 * length * width * 2),
    )
    return pl.pallas_call(
        attention_kernel,
        out_shape=jax.ShapeDtypeStruct(query_t.shape, query_t.dtype),
        grid_spec=pltpu.PrefetchScalarGridSpec(
            num_scalar_prefetch=3,
            grid=(chunks,),
            in_specs=[
                pl.BlockSpec((1, width, rows), lambda i, *_: (i, 0, 0)),
                pl.BlockSpec((chunks, width, rows), lambda i, *_: (0, 0, 0), pipeline_mode=pl.Buffered(1)),
                pl.BlockSpec((chunks, width, rows), lambda i, *_: (0, 0, 0), pipeline_mode=pl.Buffered(1)),
                pl.BlockSpec((rows, 1), lambda i, *_: (i, 0)),
                pl.BlockSpec((chunks, 1, rows), lambda i, *_: (0, 0, 0)),
            ],
            out_specs=pl.BlockSpec((1, width, rows), lambda i, *_: (i, 0, 0)),
            scratch_shapes=[
                pltpu.VMEM((heads_here, rows, 1), jnp.float32),
                pltpu.VMEM((heads_here, rows, 1), jnp.float32),
                pltpu.VMEM((heads_here, rows, HD), jnp.float32),
                pltpu.VMEM((heads_here, rows, HD), jnp.bfloat16),
            ],
        ),
        compiler_params=pltpu.CompilerParams(dimension_semantics=("arbitrary",)),
        cost_estimate=cost,
    )(first_chunk, seg_first, seg_last, query_t, key_t, value_t, qseg, kseg)


def to_heads(rows_in):
    tok_count = lax.axis_size("tok")
    token_rows, feature_width = rows_in.shape[1], rows_in.shape[2]
    split = rows_in[0].reshape(token_rows, tok_count, feature_width // tok_count)
    gathered = lax.all_to_all(split, "tok", split_axis=1, concat_axis=1, tiled=True)
    return gathered.transpose(1, 2, 0)


def from_heads(attended_t):
    token_rows = attended_t.shape[2]
    by_source = attended_t.transpose(2, 0, 1)
    returned = lax.all_to_all(by_source, "tok", split_axis=1, concat_axis=1, tiled=True)
    return returned.reshape(1, token_rows, -1)


def relocate_by_head(cache_blocks):
    tok_count = lax.axis_size("tok")
    local_blocks = cache_blocks[0]
    block_count, kv_count, heads_all, entries = local_blocks.shape
    split = local_blocks.reshape(block_count, kv_count, tok_count, heads_all // tok_count, entries)
    return lax.all_to_all(split, "tok", split_axis=2, concat_axis=2, tiled=True)


def place_slots(by_head, targets):
    groups = lax.axis_size("req")
    block_count = by_head.shape[0]
    positions = jnp.arange(block_count, dtype=jnp.int32)
    earlier = (targets[:, :, None] == targets[:, None, :]) & (positions[None, None, :] < positions[None, :, None])
    slot_rank = jnp.sum(earlier.astype(jnp.int32), axis=2)
    group_ids = jnp.arange(groups, dtype=jnp.int32)
    slot_ids = jnp.arange(CAP, dtype=jnp.int32)
    placing = (
        (targets[:, :, None, None] == group_ids[None, None, :, None])
        & (slot_rank[:, :, None, None] == slot_ids[None, None, None, :])
    ).astype(by_head.dtype)
    return jnp.einsum(
        "tbgc,bktjy->gcktjy", placing, by_head, preferred_element_type=jnp.float32
    ).astype(by_head.dtype)


def relocate_groups(outgoing):
    arrived = lax.all_to_all(outgoing, "req", split_axis=0, concat_axis=0, tiled=True)
    return arrived[None]


def on_device(query_rows, key_rows, value_rows, lengths, cache_blocks, destinations):
    span_length = query_rows.shape[1] * lax.axis_size("tok")
    segments = segment_ids(lengths[0], span_length)
    targets = lax.all_gather(destinations[0, :, 0], "tok")
    targets, cache_blocks = lax.optimization_barrier((targets, cache_blocks))
    by_head = relocate_by_head(cache_blocks)
    by_head, query_rows, key_rows, value_rows = lax.optimization_barrier(
        (by_head, query_rows, key_rows, value_rows)
    )
    outgoing = place_slots(by_head, targets)
    query_t, key_t, value_t = to_heads(query_rows), to_heads(key_rows), to_heads(value_rows)
    outgoing, query_t, key_t, value_t = lax.optimization_barrier((outgoing, query_t, key_t, value_t))
    moved_cache = relocate_groups(outgoing)
    attended_t = attend_local(query_t, key_t, value_t, lengths[0], segments)
    moved_cache, attended_t = lax.optimization_barrier((moved_cache, attended_t))
    attended = from_heads(attended_t)
    return (attended, moved_cache)


def solution(mesh):
    return jax.shard_map(
        on_device,
        mesh=mesh,
        in_specs=(
            P("req", "tok", None),
            P("req", "tok", None),
            P("req", "tok", None),
            P("req", None),
            P("req", "tok", None, None, None),
            P("req", "tok", None),
        ),
        out_specs=(P("req", "tok", None), P("req", None, None, None, None, "tok", None)),
        check_vma=False,
    )
```

```python
import functools

import jax
import jax.numpy as jnp
from jax import lax
from jax.experimental import pallas as pl
from jax.experimental.pallas import tpu as pltpu
from jax.sharding import PartitionSpec as P

HD = 224
CAP = 2
NEG = -1e30


def segment_ids(lengths_row, span_length):
    ends = jnp.cumsum(lengths_row)
    positions = jnp.arange(span_length, dtype=jnp.int32)
    return jnp.sum((positions[:, None] >= ends[None, :]).astype(jnp.int32), axis=1)


def attention_kernel(first_ref, seg_first_ref, seg_last_ref, q_ref, k_ref, v_ref, qseg_ref, kseg_ref, o_ref,
                     m_ref, l_ref, acc_ref, k_sc):
    qi = pl.program_id(0)
    chunks, width, rows = k_ref.shape
    heads_here = width // HD
    nt = (((1,), (1,)), ((), ()))

    @pl.when(qi == 0)
    def _():
        eye = (
            lax.broadcasted_iota(jnp.int32, (rows, rows), 0) == lax.broadcasted_iota(jnp.int32, (rows, rows), 1)
        ).astype(jnp.bfloat16)

        def fill(c, carry):
            start = pl.multiple_of(c * rows, rows)
            for h in range(heads_here):
                k_sc[h, pl.ds(start, rows), :] = lax.dot_general(
                    eye, k_ref[c, h * HD:(h + 1) * HD, :], nt, preferred_element_type=jnp.float32
                ).astype(jnp.bfloat16)
            return carry

        lax.fori_loop(0, chunks, fill, 0)

    m_ref[...] = jnp.full(m_ref.shape, NEG, jnp.float32)
    l_ref[...] = jnp.zeros(l_ref.shape, jnp.float32)
    acc_ref[...] = jnp.zeros(acc_ref.shape, jnp.float32)
    scale = HD ** (-0.5)
    query_seg = qseg_ref[...]
    query_pos = qi * rows + lax.broadcasted_iota(jnp.int32, (1, rows), 1)

    def step(kb, masked):
        start = pl.multiple_of(kb * rows, rows)
        if masked:
            key_seg = kseg_ref[pl.ds(start, rows), :]
            key_pos = start + lax.broadcasted_iota(jnp.int32, (rows, 1), 0)
            visible = (key_seg == query_seg) & (key_pos <= query_pos)
        for h in range(heads_here):
            keys = k_sc[h, pl.ds(start, rows), :]
            scores = jnp.dot(keys, q_ref[0, h * HD:(h + 1) * HD, :], preferred_element_type=jnp.float32) * scale
            if masked:
                scores = jnp.where(visible, scores, NEG)
            m_old = m_ref[h]
            m_new = jnp.maximum(m_old, jnp.max(scores, axis=0, keepdims=True))
            alpha = jnp.exp(m_old - m_new)
            weights = jnp.exp(scores - m_new)
            if masked:
                weights = jnp.where(visible, weights, 0.0)
            l_ref[h] = alpha * l_ref[h] + jnp.sum(weights, axis=0, keepdims=True)
            m_ref[h] = m_new
            values = v_ref[kb, h * HD:(h + 1) * HD, :]
            acc_ref[h] = alpha * acc_ref[h] + jnp.dot(
                values, weights.astype(jnp.bfloat16), preferred_element_type=jnp.float32
            )

    def body(kb, carry):
        full = (kb < qi) & (seg_first_ref[kb] == seg_last_ref[qi])

        @pl.when(full)
        def _():
            step(kb, False)

        @pl.when(jnp.logical_not(full))
        def _():
            step(kb, True)

        return carry

    lax.fori_loop(first_ref[qi], qi + 1, body, 0)
    for h in range(heads_here):
        o_ref[0, h * HD:(h + 1) * HD, :] = (acc_ref[h] / l_ref[h]).astype(o_ref.dtype)


def attend_local(query_t, key_t, value_t, lengths_row, segments):
    chunks, width, rows = query_t.shape
    heads_here = width // HD
    length = chunks * rows
    ends = jnp.cumsum(lengths_row)
    starts = ends - lengths_row
    seg_first = segments[::rows]
    seg_last = segments[rows - 1::rows]
    first_start = jnp.sum(
        jnp.where(seg_first[:, None] == jnp.arange(lengths_row.shape[0])[None, :], starts[None, :], 0), axis=1
    )
    first_chunk = (first_start // rows).astype(jnp.int32)
    qseg = segments.reshape(chunks, 1, rows)
    kseg = segments.reshape(length, 1)
    visible_pairs = length * length // 2
    cost = pl.CostEstimate(
        flops=int(4 * visible_pairs * width),
        transcendentals=int(heads_here * visible_pairs),
        bytes_accessed=int(4 * length * width * 2),
    )
    return pl.pallas_call(
        attention_kernel,
        out_shape=jax.ShapeDtypeStruct(query_t.shape, query_t.dtype),
        grid_spec=pltpu.PrefetchScalarGridSpec(
            num_scalar_prefetch=3,
            grid=(chunks,),
            in_specs=[
                pl.BlockSpec((1, width, rows), lambda i, *_: (i, 0, 0)),
                pl.BlockSpec((chunks, width, rows), lambda i, *_: (0, 0, 0), pipeline_mode=pl.Buffered(1)),
                pl.BlockSpec((chunks, width, rows), lambda i, *_: (0, 0, 0), pipeline_mode=pl.Buffered(1)),
                pl.BlockSpec((None, 1, rows), lambda i, *_: (i, 0, 0)),
                pl.BlockSpec((length, 1), lambda i, *_: (0, 0), pipeline_mode=pl.Buffered(1)),
            ],
            out_specs=pl.BlockSpec((1, width, rows), lambda i, *_: (i, 0, 0)),
            scratch_shapes=[
                pltpu.VMEM((heads_here, 1, rows), jnp.float32),
                pltpu.VMEM((heads_here, 1, rows), jnp.float32),
                pltpu.VMEM((heads_here, HD, rows), jnp.float32),
                pltpu.VMEM((heads_here, length, HD), jnp.bfloat16),
            ],
        ),
        compiler_params=pltpu.CompilerParams(dimension_semantics=("arbitrary",)),
        cost_estimate=cost,
    )(first_chunk, seg_first, seg_last, query_t, key_t, value_t, qseg, kseg)


def to_heads(rows_in):
    tok_count = lax.axis_size("tok")
    token_rows, feature_width = rows_in.shape[1], rows_in.shape[2]
    split = rows_in[0].reshape(token_rows, tok_count, feature_width // tok_count)
    gathered = lax.all_to_all(split, "tok", split_axis=1, concat_axis=1, tiled=True)
    return gathered.transpose(1, 2, 0)


def from_heads(attended_t):
    token_rows = attended_t.shape[2]
    by_source = attended_t.transpose(2, 0, 1)
    returned = lax.all_to_all(by_source, "tok", split_axis=1, concat_axis=1, tiled=True)
    return returned.reshape(1, token_rows, -1)


def relocate_by_head(cache_blocks):
    tok_count = lax.axis_size("tok")
    local_blocks = cache_blocks[0]
    block_count, kv_count, heads_all, entries = local_blocks.shape
    split = local_blocks.reshape(block_count, kv_count, tok_count, heads_all // tok_count, entries)
    return lax.all_to_all(split, "tok", split_axis=2, concat_axis=2, tiled=True)


def place_slots(by_head, targets):
    groups = lax.axis_size("req")
    block_count = by_head.shape[0]
    positions = jnp.arange(block_count, dtype=jnp.int32)
    earlier = (targets[:, :, None] == targets[:, None, :]) & (positions[None, None, :] < positions[None, :, None])
    slot_rank = jnp.sum(earlier.astype(jnp.int32), axis=2)
    group_ids = jnp.arange(groups, dtype=jnp.int32)
    slot_ids = jnp.arange(CAP, dtype=jnp.int32)
    placing = (
        (targets[:, :, None, None] == group_ids[None, None, :, None])
        & (slot_rank[:, :, None, None] == slot_ids[None, None, None, :])
    ).astype(by_head.dtype)
    return jnp.einsum(
        "tbgc,bktjy->gcktjy", placing, by_head, preferred_element_type=jnp.float32
    ).astype(by_head.dtype)


def relocate_groups(outgoing):
    arrived = lax.all_to_all(outgoing, "req", split_axis=0, concat_axis=0, tiled=True)
    return arrived[None]


def on_device(query_rows, key_rows, value_rows, lengths, cache_blocks, destinations):
    span_length = query_rows.shape[1] * lax.axis_size("tok")
    segments = segment_ids(lengths[0], span_length)
    tok_count = lax.axis_size("tok")
    own_targets = destinations[0, :, 0]
    targets = lax.all_to_all(
        jnp.broadcast_to(own_targets[None, :], (tok_count, own_targets.shape[0])),
        "tok", split_axis=0, concat_axis=0, tiled=True,
    )
    targets, cache_blocks = lax.optimization_barrier((targets, cache_blocks))
    by_head = relocate_by_head(cache_blocks)
    by_head, query_rows, key_rows, value_rows = lax.optimization_barrier(
        (by_head, query_rows, key_rows, value_rows)
    )
    outgoing = place_slots(by_head, targets)
    query_t, key_t, value_t = to_heads(query_rows), to_heads(key_rows), to_heads(value_rows)
    outgoing, query_t, key_t, value_t = lax.optimization_barrier((outgoing, query_t, key_t, value_t))
    moved_cache = relocate_groups(outgoing)
    attended_t = attend_local(query_t, key_t, value_t, lengths[0], segments)
    moved_cache, attended_t = lax.optimization_barrier((moved_cache, attended_t))
    attended = from_heads(attended_t)
    return (attended, moved_cache)


def solution(mesh):
    return jax.shard_map(
        on_device,
        mesh=mesh,
        in_specs=(
            P("req", "tok", None),
            P("req", "tok", None),
            P("req", "tok", None),
            P("req", None),
            P("req", "tok", None, None, None),
            P("req", "tok", None),
        ),
        out_specs=(P("req", "tok", None), P("req", None, None, None, None, "tok", None)),
        check_vma=False,
    )
```

```python
import functools

import jax
import jax.numpy as jnp
from jax import lax
from jax.experimental import pallas as pl
from jax.experimental.pallas import tpu as pltpu
from jax.sharding import PartitionSpec as P

HD = 224
CAP = 2
NEG = -1e30


def segment_ids(lengths_row, span_length):
    ends = jnp.cumsum(lengths_row)
    positions = jnp.arange(span_length, dtype=jnp.int32)
    return jnp.sum((positions[:, None] >= ends[None, :]).astype(jnp.int32), axis=1)


def attention_kernel(first_ref, seg_first_ref, seg_last_ref, q_ref, k_ref, v_ref, qseg_ref, kseg_ref, o_ref,
                     m_ref, l_ref, acc_ref, k_sc):
    qi = pl.program_id(0)
    chunks, width, rows = k_ref.shape
    heads_here = width // HD
    nt = (((1,), (1,)), ((), ()))

    @pl.when(qi == 0)
    def _():
        eye = (
            lax.broadcasted_iota(jnp.int32, (rows, rows), 0) == lax.broadcasted_iota(jnp.int32, (rows, rows), 1)
        ).astype(jnp.bfloat16)

        def fill(c, carry):
            start = pl.multiple_of(c * rows, rows)
            for h in range(heads_here):
                k_sc[h, pl.ds(start, rows), :] = lax.dot_general(
                    eye, k_ref[c, h * HD:(h + 1) * HD, :], nt, preferred_element_type=jnp.float32
                ).astype(jnp.bfloat16)
            return carry

        lax.fori_loop(0, chunks, fill, 0)

    m_ref[...] = jnp.full(m_ref.shape, NEG, jnp.float32)
    l_ref[...] = jnp.zeros(l_ref.shape, jnp.float32)
    acc_ref[...] = jnp.zeros(acc_ref.shape, jnp.float32)
    scale = HD ** (-0.5)
    query_seg = qseg_ref[...]
    query_pos = qi * rows + lax.broadcasted_iota(jnp.int32, (1, rows), 1)

    def step(kb, masked):
        start = pl.multiple_of(kb * rows, rows)
        if masked:
            key_seg = kseg_ref[pl.ds(start, rows), :]
            key_pos = start + lax.broadcasted_iota(jnp.int32, (rows, 1), 0)
            visible = (key_seg == query_seg) & (key_pos <= query_pos)
        for h in range(heads_here):
            keys = k_sc[h, pl.ds(start, rows), :]
            scores = jnp.dot(keys, q_ref[0, h * HD:(h + 1) * HD, :], preferred_element_type=jnp.float32) * scale
            if masked:
                scores = jnp.where(visible, scores, NEG)
            m_old = m_ref[h]
            m_new = jnp.maximum(m_old, jnp.max(scores, axis=0, keepdims=True))
            alpha = jnp.exp(m_old - m_new)
            weights = jnp.exp(scores - m_new)
            if masked:
                weights = jnp.where(visible, weights, 0.0)
            l_ref[h] = alpha * l_ref[h] + jnp.sum(weights, axis=0, keepdims=True)
            m_ref[h] = m_new
            values = v_ref[kb, h * HD:(h + 1) * HD, :]
            acc_ref[h] = alpha * acc_ref[h] + jnp.dot(
                values, weights.astype(jnp.bfloat16), preferred_element_type=jnp.float32
            )

    def body(kb, carry):
        full = (kb < qi) & (seg_first_ref[kb] == seg_last_ref[qi])

        @pl.when(full)
        def _():
            step(kb, False)

        @pl.when(jnp.logical_not(full))
        def _():
            step(kb, True)

        return carry

    lax.fori_loop(first_ref[qi], qi + 1, body, 0)
    for h in range(heads_here):
        o_ref[0, h * HD:(h + 1) * HD, :] = (acc_ref[h] / l_ref[h]).astype(o_ref.dtype)


def attend_local(query_t, key_t, value_t, lengths_row, segments):
    chunks, width, rows = query_t.shape
    heads_here = width // HD
    length = chunks * rows
    ends = jnp.cumsum(lengths_row)
    starts = ends - lengths_row
    seg_first = segments[::rows]
    seg_last = segments[rows - 1::rows]
    first_start = jnp.sum(
        jnp.where(seg_first[:, None] == jnp.arange(lengths_row.shape[0])[None, :], starts[None, :], 0), axis=1
    )
    first_chunk = (first_start // rows).astype(jnp.int32)
    qseg = segments.reshape(chunks, 1, rows)
    kseg = segments.reshape(length, 1)
    visible_pairs = length * length // 2
    cost = pl.CostEstimate(
        flops=int(4 * visible_pairs * width),
        transcendentals=int(heads_here * visible_pairs),
        bytes_accessed=int(4 * length * width * 2),
    )
    return pl.pallas_call(
        attention_kernel,
        out_shape=jax.ShapeDtypeStruct(query_t.shape, query_t.dtype),
        grid_spec=pltpu.PrefetchScalarGridSpec(
            num_scalar_prefetch=3,
            grid=(chunks,),
            in_specs=[
                pl.BlockSpec((1, width, rows), lambda i, *_: (i, 0, 0)),
                pl.BlockSpec((chunks, width, rows), lambda i, *_: (0, 0, 0), pipeline_mode=pl.Buffered(1)),
                pl.BlockSpec((chunks, width, rows), lambda i, *_: (0, 0, 0), pipeline_mode=pl.Buffered(1)),
                pl.BlockSpec((None, 1, rows), lambda i, *_: (i, 0, 0)),
                pl.BlockSpec((length, 1), lambda i, *_: (0, 0), pipeline_mode=pl.Buffered(1)),
            ],
            out_specs=pl.BlockSpec((1, width, rows), lambda i, *_: (i, 0, 0)),
            scratch_shapes=[
                pltpu.VMEM((heads_here, 1, rows), jnp.float32),
                pltpu.VMEM((heads_here, 1, rows), jnp.float32),
                pltpu.VMEM((heads_here, HD, rows), jnp.float32),
                pltpu.VMEM((heads_here, length, HD), jnp.bfloat16),
            ],
        ),
        compiler_params=pltpu.CompilerParams(dimension_semantics=("arbitrary",)),
        cost_estimate=cost,
    )(first_chunk, seg_first, seg_last, query_t, key_t, value_t, qseg, kseg)


def to_heads(rows_in):
    tok_count = lax.axis_size("tok")
    token_rows, feature_width = rows_in.shape[1], rows_in.shape[2]
    split = rows_in[0].reshape(token_rows, tok_count, feature_width // tok_count)
    gathered = lax.all_to_all(split, "tok", split_axis=1, concat_axis=1, tiled=True)
    return gathered.transpose(1, 2, 0)


def from_heads(attended_t):
    token_rows = attended_t.shape[2]
    by_source = attended_t.transpose(2, 0, 1)
    returned = lax.all_to_all(by_source, "tok", split_axis=1, concat_axis=1, tiled=True)
    return returned.reshape(1, token_rows, -1)


def relocate_by_head(cache_blocks):
    tok_count = lax.axis_size("tok")
    local_blocks = cache_blocks[0]
    block_count, kv_count, heads_all, entries = local_blocks.shape
    split = local_blocks.reshape(block_count, kv_count, tok_count, heads_all // tok_count, entries)
    return lax.all_to_all(split, "tok", split_axis=2, concat_axis=2, tiled=True)


def place_slots(by_head, targets):
    groups = lax.axis_size("req")
    block_count = by_head.shape[0]
    positions = jnp.arange(block_count, dtype=jnp.int32)
    earlier = (targets[:, :, None] == targets[:, None, :]) & (positions[None, None, :] < positions[None, :, None])
    slot_rank = jnp.sum(earlier.astype(jnp.int32), axis=2)
    group_ids = jnp.arange(groups, dtype=jnp.int32)
    slot_ids = jnp.arange(CAP, dtype=jnp.int32)
    placing = (
        (targets[:, :, None, None] == group_ids[None, None, :, None])
        & (slot_rank[:, :, None, None] == slot_ids[None, None, None, :])
    ).astype(by_head.dtype)
    return jnp.einsum(
        "tbgc,bktjy->gcktjy", placing, by_head, preferred_element_type=jnp.float32
    ).astype(by_head.dtype)


def relocate_groups(outgoing):
    arrived = lax.all_to_all(outgoing, "req", split_axis=0, concat_axis=0, tiled=True)
    return arrived[None]


def on_device(query_rows, key_rows, value_rows, lengths, cache_blocks, destinations):
    span_length = query_rows.shape[1] * lax.axis_size("tok")
    segments = segment_ids(lengths[0], span_length)
    tok_count = lax.axis_size("tok")
    own_targets = destinations[0, :, 0]
    targets = lax.all_to_all(
        jnp.broadcast_to(own_targets[None, :], (tok_count, own_targets.shape[0])),
        "tok", split_axis=0, concat_axis=0, tiled=True,
    )
    query_t = to_heads(query_rows)
    by_head = relocate_by_head(cache_blocks)
    by_head, key_rows, value_rows = lax.optimization_barrier((by_head, key_rows, value_rows))
    outgoing = place_slots(by_head, targets)
    key_t, value_t = to_heads(key_rows), to_heads(value_rows)
    outgoing, query_t, key_t, value_t = lax.optimization_barrier((outgoing, query_t, key_t, value_t))
    moved_cache = relocate_groups(outgoing)
    attended_t = attend_local(query_t, key_t, value_t, lengths[0], segments)
    moved_cache, attended_t = lax.optimization_barrier((moved_cache, attended_t))
    attended = from_heads(attended_t)
    return (attended, moved_cache)


def solution(mesh):
    return jax.shard_map(
        on_device,
        mesh=mesh,
        in_specs=(
            P("req", "tok", None),
            P("req", "tok", None),
            P("req", "tok", None),
            P("req", None),
            P("req", "tok", None, None, None),
            P("req", "tok", None),
        ),
        out_specs=(P("req", "tok", None), P("req", None, None, None, None, "tok", None)),
        check_vma=False,
    )
```

```python
import functools

import jax
import jax.numpy as jnp
from jax import lax
from jax.experimental import pallas as pl
from jax.experimental.pallas import tpu as pltpu
from jax.sharding import PartitionSpec as P

HD = 224
CAP = 2
NEG = -1e30


def segment_ids(lengths_row, span_length):
    ends = jnp.cumsum(lengths_row)
    positions = jnp.arange(span_length, dtype=jnp.int32)
    return jnp.sum((positions[:, None] >= ends[None, :]).astype(jnp.int32), axis=1)


def attention_kernel(first_ref, seg_first_ref, seg_last_ref, q_ref, k_ref, v_ref, qseg_ref, kseg_ref, o_ref,
                     m_ref, l_ref, acc_ref, k_sc):
    qi = pl.program_id(0)
    chunks, width, rows = k_ref.shape
    heads_here = width // HD
    nt = (((1,), (1,)), ((), ()))

    @pl.when(qi == 0)
    def _():
        eye = (
            lax.broadcasted_iota(jnp.int32, (rows, rows), 0) == lax.broadcasted_iota(jnp.int32, (rows, rows), 1)
        ).astype(jnp.bfloat16)

        def fill(c, carry):
            start = pl.multiple_of(c * rows, rows)
            for h in range(heads_here):
                k_sc[h, pl.ds(start, rows), :] = lax.dot_general(
                    eye, k_ref[c, h * HD:(h + 1) * HD, :], nt, preferred_element_type=jnp.float32
                ).astype(jnp.bfloat16)
            return carry

        lax.fori_loop(0, chunks, fill, 0)

    m_ref[...] = jnp.full(m_ref.shape, NEG, jnp.float32)
    l_ref[...] = jnp.zeros(l_ref.shape, jnp.float32)
    acc_ref[...] = jnp.zeros(acc_ref.shape, jnp.float32)
    scale = HD ** (-0.5)
    query_seg = qseg_ref[...]
    query_pos = qi * rows + lax.broadcasted_iota(jnp.int32, (1, rows), 1)

    def step(kb, masked):
        start = pl.multiple_of(kb * rows, rows)
        if masked:
            key_seg = kseg_ref[pl.ds(start, rows), :]
            key_pos = start + lax.broadcasted_iota(jnp.int32, (rows, 1), 0)
            visible = (key_seg == query_seg) & (key_pos <= query_pos)
        for h in range(heads_here):
            keys = k_sc[h, pl.ds(start, rows), :]
            scores = jnp.dot(keys, q_ref[0, h * HD:(h + 1) * HD, :], preferred_element_type=jnp.float32) * scale
            if masked:
                scores = jnp.where(visible, scores, NEG)
            m_old = m_ref[h]
            m_new = jnp.maximum(m_old, jnp.max(scores, axis=0, keepdims=True))
            alpha = jnp.exp(m_old - m_new)
            weights = jnp.exp(scores - m_new)
            if masked:
                weights = jnp.where(visible, weights, 0.0)
            l_ref[h] = alpha * l_ref[h] + jnp.sum(weights, axis=0, keepdims=True)
            m_ref[h] = m_new
            values = v_ref[kb, h * HD:(h + 1) * HD, :]
            acc_ref[h] = alpha * acc_ref[h] + jnp.dot(
                values, weights.astype(jnp.bfloat16), preferred_element_type=jnp.float32
            )

    def body(kb, carry):
        full = (kb < qi) & (seg_first_ref[kb] == seg_last_ref[qi])

        @pl.when(full)
        def _():
            step(kb, False)

        @pl.when(jnp.logical_not(full))
        def _():
            step(kb, True)

        return carry

    lax.fori_loop(first_ref[qi], qi + 1, body, 0)
    for h in range(heads_here):
        o_ref[0, h * HD:(h + 1) * HD, :] = (acc_ref[h] / l_ref[h]).astype(o_ref.dtype)


def attend_local(query_t, key_t, value_t, lengths_row, segments):
    chunks, width, rows = query_t.shape
    heads_here = width // HD
    length = chunks * rows
    ends = jnp.cumsum(lengths_row)
    starts = ends - lengths_row
    seg_first = segments[::rows]
    seg_last = segments[rows - 1::rows]
    first_start = jnp.sum(
        jnp.where(seg_first[:, None] == jnp.arange(lengths_row.shape[0])[None, :], starts[None, :], 0), axis=1
    )
    first_chunk = (first_start // rows).astype(jnp.int32)
    qseg = segments.reshape(chunks, 1, rows)
    kseg = segments.reshape(length, 1)
    visible_pairs = length * length // 2
    cost = pl.CostEstimate(
        flops=int(4 * visible_pairs * width),
        transcendentals=int(heads_here * visible_pairs),
        bytes_accessed=int(4 * length * width * 2),
    )
    return pl.pallas_call(
        attention_kernel,
        out_shape=jax.ShapeDtypeStruct(query_t.shape, query_t.dtype),
        grid_spec=pltpu.PrefetchScalarGridSpec(
            num_scalar_prefetch=3,
            grid=(chunks,),
            in_specs=[
                pl.BlockSpec((1, width, rows), lambda i, *_: (i, 0, 0)),
                pl.BlockSpec((chunks, width, rows), lambda i, *_: (0, 0, 0), pipeline_mode=pl.Buffered(1)),
                pl.BlockSpec((chunks, width, rows), lambda i, *_: (0, 0, 0), pipeline_mode=pl.Buffered(1)),
                pl.BlockSpec((None, 1, rows), lambda i, *_: (i, 0, 0)),
                pl.BlockSpec((length, 1), lambda i, *_: (0, 0), pipeline_mode=pl.Buffered(1)),
            ],
            out_specs=pl.BlockSpec((1, width, rows), lambda i, *_: (i, 0, 0)),
            scratch_shapes=[
                pltpu.VMEM((heads_here, 1, rows), jnp.float32),
                pltpu.VMEM((heads_here, 1, rows), jnp.float32),
                pltpu.VMEM((heads_here, HD, rows), jnp.float32),
                pltpu.VMEM((heads_here, length, HD), jnp.bfloat16),
            ],
        ),
        compiler_params=pltpu.CompilerParams(dimension_semantics=("arbitrary",)),
        cost_estimate=cost,
    )(first_chunk, seg_first, seg_last, query_t, key_t, value_t, qseg, kseg)


def to_heads(rows_in):
    tok_count = lax.axis_size("tok")
    token_rows, feature_width = rows_in.shape[1], rows_in.shape[2]
    split = rows_in[0].reshape(token_rows, tok_count, feature_width // tok_count)
    gathered = lax.all_to_all(split, "tok", split_axis=1, concat_axis=1, tiled=True)
    return gathered.transpose(1, 2, 0)


def from_heads(attended_t):
    token_rows = attended_t.shape[2]
    by_source = attended_t.transpose(2, 0, 1)
    returned = lax.all_to_all(by_source, "tok", split_axis=1, concat_axis=1, tiled=True)
    return returned.reshape(1, token_rows, -1)


def relocate_by_head(cache_blocks):
    tok_count = lax.axis_size("tok")
    local_blocks = cache_blocks[0]
    block_count, kv_count, heads_all, entries = local_blocks.shape
    split = local_blocks.reshape(block_count, kv_count, tok_count, heads_all // tok_count, entries)
    return lax.all_to_all(split, "tok", split_axis=2, concat_axis=2, tiled=True)


def place_slots(by_head, targets):
    groups = lax.axis_size("req")
    block_count = by_head.shape[0]
    positions = jnp.arange(block_count, dtype=jnp.int32)
    earlier = (targets[:, :, None] == targets[:, None, :]) & (positions[None, None, :] < positions[None, :, None])
    slot_rank = jnp.sum(earlier.astype(jnp.int32), axis=2)
    group_ids = jnp.arange(groups, dtype=jnp.int32)
    slot_ids = jnp.arange(CAP, dtype=jnp.int32)
    placing = (
        (targets[:, :, None, None] == group_ids[None, None, :, None])
        & (slot_rank[:, :, None, None] == slot_ids[None, None, None, :])
    ).astype(by_head.dtype)
    return jnp.einsum(
        "tbgc,bktjy->gcktjy", placing, by_head, preferred_element_type=jnp.float32
    ).astype(by_head.dtype)


def relocate_groups(outgoing):
    arrived = lax.all_to_all(outgoing, "req", split_axis=0, concat_axis=0, tiled=True)
    return arrived[None]


def on_device(query_rows, key_rows, value_rows, lengths, cache_blocks, destinations):
    span_length = query_rows.shape[1] * lax.axis_size("tok")
    segments = segment_ids(lengths[0], span_length)
    tok_count = lax.axis_size("tok")
    query_t = to_heads(query_rows)
    query_t, destinations = lax.optimization_barrier((query_t, destinations))
    own_targets = destinations[0, :, 0]
    targets = lax.all_to_all(
        jnp.broadcast_to(own_targets[None, :], (tok_count, own_targets.shape[0])),
        "tok", split_axis=0, concat_axis=0, tiled=True,
    )
    by_head = relocate_by_head(cache_blocks)
    by_head, key_rows, value_rows = lax.optimization_barrier((by_head, key_rows, value_rows))
    outgoing = place_slots(by_head, targets)
    key_t, value_t = to_heads(key_rows), to_heads(value_rows)
    outgoing, query_t, key_t, value_t = lax.optimization_barrier((outgoing, query_t, key_t, value_t))
    moved_cache = relocate_groups(outgoing)
    attended_t = attend_local(query_t, key_t, value_t, lengths[0], segments)
    moved_cache, attended_t = lax.optimization_barrier((moved_cache, attended_t))
    attended = from_heads(attended_t)
    return (attended, moved_cache)


def solution(mesh):
    return jax.shard_map(
        on_device,
        mesh=mesh,
        in_specs=(
            P("req", "tok", None),
            P("req", "tok", None),
            P("req", "tok", None),
            P("req", None),
            P("req", "tok", None, None, None),
            P("req", "tok", None),
        ),
        out_specs=(P("req", "tok", None), P("req", None, None, None, None, "tok", None)),
        check_vma=False,
    )
```

```python
import functools

import jax
import jax.numpy as jnp
from jax import lax
from jax.experimental import pallas as pl
from jax.experimental.pallas import tpu as pltpu
from jax.sharding import PartitionSpec as P

HD = 224
CAP = 2
NEG = -1e30


def segment_ids(lengths_row, span_length):
    ends = jnp.cumsum(lengths_row)
    positions = jnp.arange(span_length, dtype=jnp.int32)
    return jnp.sum((positions[:, None] >= ends[None, :]).astype(jnp.int32), axis=1)


def attention_kernel(first_ref, seg_first_ref, seg_last_ref, q_ref, k_ref, v_ref, qseg_ref, kseg_ref, o_ref,
                     m_ref, l_ref, acc_ref, k_sc):
    qi = pl.program_id(0)
    chunks, width, rows = k_ref.shape
    heads_here = width // HD
    nt = (((1,), (1,)), ((), ()))

    @pl.when(qi == 0)
    def _():
        eye = (
            lax.broadcasted_iota(jnp.int32, (rows, rows), 0) == lax.broadcasted_iota(jnp.int32, (rows, rows), 1)
        ).astype(jnp.bfloat16)

        def fill(c, carry):
            start = pl.multiple_of(c * rows, rows)
            for h in range(heads_here):
                k_sc[h, pl.ds(start, rows), :] = lax.dot_general(
                    eye, k_ref[c, h * HD:(h + 1) * HD, :], nt, preferred_element_type=jnp.float32
                ).astype(jnp.bfloat16)
            return carry

        lax.fori_loop(0, chunks, fill, 0)

    m_ref[...] = jnp.full(m_ref.shape, NEG, jnp.float32)
    l_ref[...] = jnp.zeros(l_ref.shape, jnp.float32)
    acc_ref[...] = jnp.zeros(acc_ref.shape, jnp.float32)
    scale = HD ** (-0.5)
    query_seg = qseg_ref[...]
    query_pos = qi * rows + lax.broadcasted_iota(jnp.int32, (1, rows), 1)

    def step(kb, masked):
        start = pl.multiple_of(kb * rows, rows)
        if masked:
            key_seg = kseg_ref[pl.ds(start, rows), :]
            key_pos = start + lax.broadcasted_iota(jnp.int32, (rows, 1), 0)
            visible = (key_seg == query_seg) & (key_pos <= query_pos)
        for h in range(heads_here):
            keys = k_sc[h, pl.ds(start, rows), :]
            scores = jnp.dot(keys, q_ref[0, h * HD:(h + 1) * HD, :], preferred_element_type=jnp.float32) * scale
            if masked:
                scores = jnp.where(visible, scores, NEG)
            m_old = m_ref[h]
            m_new = jnp.maximum(m_old, jnp.max(scores, axis=0, keepdims=True))
            alpha = jnp.exp(m_old - m_new)
            weights = jnp.exp(scores - m_new)
            if masked:
                weights = jnp.where(visible, weights, 0.0)
            l_ref[h] = alpha * l_ref[h] + jnp.sum(weights, axis=0, keepdims=True)
            m_ref[h] = m_new
            values = v_ref[kb, h * HD:(h + 1) * HD, :]
            acc_ref[h] = alpha * acc_ref[h] + jnp.dot(
                values, weights.astype(jnp.bfloat16), preferred_element_type=jnp.float32
            )

    def body(kb, carry):
        full = (kb < qi) & (seg_first_ref[kb] == seg_last_ref[qi])

        @pl.when(full)
        def _():
            step(kb, False)

        @pl.when(jnp.logical_not(full))
        def _():
            step(kb, True)

        return carry

    lax.fori_loop(first_ref[qi], qi + 1, body, 0)
    for h in range(heads_here):
        o_ref[0, h * HD:(h + 1) * HD, :] = (acc_ref[h] / l_ref[h]).astype(o_ref.dtype)


def attend_local(query_t, key_t, value_t, lengths_row, segments):
    chunks, width, rows = query_t.shape
    heads_here = width // HD
    length = chunks * rows
    ends = jnp.cumsum(lengths_row)
    starts = ends - lengths_row
    seg_first = segments[::rows]
    seg_last = segments[rows - 1::rows]
    first_start = jnp.sum(
        jnp.where(seg_first[:, None] == jnp.arange(lengths_row.shape[0])[None, :], starts[None, :], 0), axis=1
    )
    first_chunk = (first_start // rows).astype(jnp.int32)
    qseg = segments.reshape(chunks, 1, rows)
    kseg = segments.reshape(length, 1)
    visible_pairs = length * length // 2
    cost = pl.CostEstimate(
        flops=int(4 * visible_pairs * width),
        transcendentals=int(heads_here * visible_pairs),
        bytes_accessed=int(4 * length * width * 2),
    )
    return pl.pallas_call(
        attention_kernel,
        out_shape=jax.ShapeDtypeStruct(query_t.shape, query_t.dtype),
        grid_spec=pltpu.PrefetchScalarGridSpec(
            num_scalar_prefetch=3,
            grid=(chunks,),
            in_specs=[
                pl.BlockSpec((1, width, rows), lambda i, *_: (i, 0, 0)),
                pl.BlockSpec((chunks, width, rows), lambda i, *_: (0, 0, 0), pipeline_mode=pl.Buffered(1)),
                pl.BlockSpec((chunks, width, rows), lambda i, *_: (0, 0, 0), pipeline_mode=pl.Buffered(1)),
                pl.BlockSpec((None, 1, rows), lambda i, *_: (i, 0, 0)),
                pl.BlockSpec((length, 1), lambda i, *_: (0, 0), pipeline_mode=pl.Buffered(1)),
            ],
            out_specs=pl.BlockSpec((1, width, rows), lambda i, *_: (i, 0, 0)),
            scratch_shapes=[
                pltpu.VMEM((heads_here, 1, rows), jnp.float32),
                pltpu.VMEM((heads_here, 1, rows), jnp.float32),
                pltpu.VMEM((heads_here, HD, rows), jnp.float32),
                pltpu.VMEM((heads_here, length, HD), jnp.bfloat16),
            ],
        ),
        compiler_params=pltpu.CompilerParams(dimension_semantics=("arbitrary",)),
        cost_estimate=cost,
    )(first_chunk, seg_first, seg_last, query_t, key_t, value_t, qseg, kseg)


def to_heads(rows_in):
    tok_count = lax.axis_size("tok")
    token_rows, feature_width = rows_in.shape[1], rows_in.shape[2]
    split = rows_in[0].reshape(token_rows, tok_count, feature_width // tok_count)
    gathered = lax.all_to_all(split, "tok", split_axis=1, concat_axis=1, tiled=True)
    return gathered.transpose(1, 2, 0)


def from_heads(attended_t):
    token_rows = attended_t.shape[2]
    by_source = attended_t.transpose(2, 0, 1)
    returned = lax.all_to_all(by_source, "tok", split_axis=1, concat_axis=1, tiled=True)
    return returned.reshape(1, token_rows, -1)


def relocate_by_head(cache_blocks):
    tok_count = lax.axis_size("tok")
    local_blocks = cache_blocks[0]
    block_count, kv_count, heads_all, entries = local_blocks.shape
    split = local_blocks.reshape(block_count, kv_count, tok_count, heads_all // tok_count, entries)
    return lax.all_to_all(split, "tok", split_axis=2, concat_axis=2, tiled=True)


def place_slots(by_head, targets):
    groups = lax.axis_size("req")
    block_count = by_head.shape[0]
    positions = jnp.arange(block_count, dtype=jnp.int32)
    earlier = (targets[:, :, None] == targets[:, None, :]) & (positions[None, None, :] < positions[None, :, None])
    slot_rank = jnp.sum(earlier.astype(jnp.int32), axis=2)
    group_ids = jnp.arange(groups, dtype=jnp.int32)
    slot_ids = jnp.arange(CAP, dtype=jnp.int32)
    match = (
        (targets.T[None, None, :, :] == group_ids[:, None, None, None])
        & (slot_rank.T[None, None, :, :] == slot_ids[None, :, None, None])
    )
    picked = jnp.where(
        match[:, :, :, None, :, None, None], by_head[None, None], jnp.zeros((), by_head.dtype)
    )
    return jnp.sum(picked, axis=2, dtype=by_head.dtype)


def relocate_groups(outgoing):
    arrived = lax.all_to_all(outgoing, "req", split_axis=0, concat_axis=0, tiled=True)
    return arrived[None]


def on_device(query_rows, key_rows, value_rows, lengths, cache_blocks, destinations):
    span_length = query_rows.shape[1] * lax.axis_size("tok")
    segments = segment_ids(lengths[0], span_length)
    tok_count = lax.axis_size("tok")
    query_t = to_heads(query_rows)
    query_t, destinations = lax.optimization_barrier((query_t, destinations))
    own_targets = destinations[0, :, 0]
    targets = lax.all_to_all(
        jnp.broadcast_to(own_targets[None, :], (tok_count, own_targets.shape[0])),
        "tok", split_axis=0, concat_axis=0, tiled=True,
    )
    by_head = relocate_by_head(cache_blocks)
    by_head, key_rows, value_rows = lax.optimization_barrier((by_head, key_rows, value_rows))
    outgoing = place_slots(by_head, targets)
    key_t, value_t = to_heads(key_rows), to_heads(value_rows)
    outgoing, query_t, key_t, value_t = lax.optimization_barrier((outgoing, query_t, key_t, value_t))
    moved_cache = relocate_groups(outgoing)
    attended_t = attend_local(query_t, key_t, value_t, lengths[0], segments)
    moved_cache, attended_t = lax.optimization_barrier((moved_cache, attended_t))
    attended = from_heads(attended_t)
    return (attended, moved_cache)


def solution(mesh):
    return jax.shard_map(
        on_device,
        mesh=mesh,
        in_specs=(
            P("req", "tok", None),
            P("req", "tok", None),
            P("req", "tok", None),
            P("req", None),
            P("req", "tok", None, None, None),
            P("req", "tok", None),
        ),
        out_specs=(P("req", "tok", None), P("req", None, None, None, None, "tok", None)),
        check_vma=False,
    )
```

```python
import functools

import jax
import jax.numpy as jnp
from jax import lax
from jax.experimental import pallas as pl
from jax.experimental.pallas import tpu as pltpu
from jax.sharding import PartitionSpec as P

HD = 224
CAP = 2
NEG = -1e30


def segment_ids(lengths_row, span_length):
    ends = jnp.cumsum(lengths_row)
    positions = jnp.arange(span_length, dtype=jnp.int32)
    return jnp.sum((positions[:, None] >= ends[None, :]).astype(jnp.int32), axis=1)


def attention_kernel(first_ref, seg_first_ref, seg_last_ref, q_ref, k_ref, v_ref, qseg_ref, kseg_ref, o_ref,
                     m_ref, l_ref, acc_ref, k_sc):
    qi = pl.program_id(0)
    chunks, width, rows = k_ref.shape
    heads_here = width // HD
    nt = (((1,), (1,)), ((), ()))

    @pl.when(qi == 0)
    def _():
        eye = (
            lax.broadcasted_iota(jnp.int32, (rows, rows), 0) == lax.broadcasted_iota(jnp.int32, (rows, rows), 1)
        ).astype(jnp.bfloat16)

        def fill(c, carry):
            start = pl.multiple_of(c * rows, rows)
            for h in range(heads_here):
                k_sc[h, pl.ds(start, rows), :] = lax.dot_general(
                    eye, k_ref[c, h * HD:(h + 1) * HD, :], nt, preferred_element_type=jnp.float32
                ).astype(jnp.bfloat16)
            return carry

        lax.fori_loop(0, chunks, fill, 0)

    m_ref[...] = jnp.full(m_ref.shape, NEG, jnp.float32)
    l_ref[...] = jnp.zeros(l_ref.shape, jnp.float32)
    acc_ref[...] = jnp.zeros(acc_ref.shape, jnp.float32)
    scale = HD ** (-0.5)
    query_seg = qseg_ref[...]
    query_pos = qi * rows + lax.broadcasted_iota(jnp.int32, (1, rows), 1)

    def step(kb, masked):
        start = pl.multiple_of(kb * rows, rows)
        if masked:
            key_seg = kseg_ref[pl.ds(start, rows), :]
            key_pos = start + lax.broadcasted_iota(jnp.int32, (rows, 1), 0)
            visible = (key_seg == query_seg) & (key_pos <= query_pos)
        for h in range(heads_here):
            keys = k_sc[h, pl.ds(start, rows), :]
            scores = jnp.dot(keys, q_ref[0, h * HD:(h + 1) * HD, :], preferred_element_type=jnp.float32) * scale
            if masked:
                scores = jnp.where(visible, scores, NEG)
            m_old = m_ref[h]
            m_new = jnp.maximum(m_old, jnp.max(scores, axis=0, keepdims=True))
            alpha = jnp.exp(m_old - m_new)
            weights = jnp.exp(scores - m_new)
            if masked:
                weights = jnp.where(visible, weights, 0.0)
            l_ref[h] = alpha * l_ref[h] + jnp.sum(weights, axis=0, keepdims=True)
            m_ref[h] = m_new
            values = v_ref[kb, h * HD:(h + 1) * HD, :]
            acc_ref[h] = alpha * acc_ref[h] + jnp.dot(
                values, weights.astype(jnp.bfloat16), preferred_element_type=jnp.float32
            )

    def body(kb, carry):
        full = (kb < qi) & (seg_first_ref[kb] == seg_last_ref[qi])

        @pl.when(full)
        def _():
            step(kb, False)

        @pl.when(jnp.logical_not(full))
        def _():
            step(kb, True)

        return carry

    lax.fori_loop(first_ref[qi], qi + 1, body, 0)
    for h in range(heads_here):
        o_ref[0, h * HD:(h + 1) * HD, :] = (acc_ref[h] / l_ref[h]).astype(o_ref.dtype)


def attend_local(query_t, key_t, value_t, lengths_row, segments):
    chunks, width, rows = query_t.shape
    heads_here = width // HD
    length = chunks * rows
    ends = jnp.cumsum(lengths_row)
    starts = ends - lengths_row
    seg_first = segments[::rows]
    seg_last = segments[rows - 1::rows]
    first_start = jnp.sum(
        jnp.where(seg_first[:, None] == jnp.arange(lengths_row.shape[0])[None, :], starts[None, :], 0), axis=1
    )
    first_chunk = (first_start // rows).astype(jnp.int32)
    qseg = segments.reshape(chunks, 1, rows)
    kseg = segments.reshape(length, 1)
    visible_pairs = length * length // 2
    cost = pl.CostEstimate(
        flops=int(4 * visible_pairs * width),
        transcendentals=int(heads_here * visible_pairs),
        bytes_accessed=int(4 * length * width * 2),
    )
    return pl.pallas_call(
        attention_kernel,
        out_shape=jax.ShapeDtypeStruct(query_t.shape, query_t.dtype),
        grid_spec=pltpu.PrefetchScalarGridSpec(
            num_scalar_prefetch=3,
            grid=(chunks,),
            in_specs=[
                pl.BlockSpec((1, width, rows), lambda i, *_: (i, 0, 0)),
                pl.BlockSpec((chunks, width, rows), lambda i, *_: (0, 0, 0), pipeline_mode=pl.Buffered(1)),
                pl.BlockSpec((chunks, width, rows), lambda i, *_: (0, 0, 0), pipeline_mode=pl.Buffered(1)),
                pl.BlockSpec((None, 1, rows), lambda i, *_: (i, 0, 0)),
                pl.BlockSpec((length, 1), lambda i, *_: (0, 0), pipeline_mode=pl.Buffered(1)),
            ],
            out_specs=pl.BlockSpec((1, width, rows), lambda i, *_: (i, 0, 0)),
            scratch_shapes=[
                pltpu.VMEM((heads_here, 1, rows), jnp.float32),
                pltpu.VMEM((heads_here, 1, rows), jnp.float32),
                pltpu.VMEM((heads_here, HD, rows), jnp.float32),
                pltpu.VMEM((heads_here, length, HD), jnp.bfloat16),
            ],
        ),
        compiler_params=pltpu.CompilerParams(dimension_semantics=("arbitrary",)),
        cost_estimate=cost,
    )(first_chunk, seg_first, seg_last, query_t, key_t, value_t, qseg, kseg)


def to_heads(rows_in):
    tok_count = lax.axis_size("tok")
    token_rows, feature_width = rows_in.shape[1], rows_in.shape[2]
    split = rows_in[0].reshape(token_rows, tok_count, feature_width // tok_count)
    gathered = lax.all_to_all(split, "tok", split_axis=1, concat_axis=1, tiled=True)
    return gathered.transpose(1, 2, 0)


def from_heads(attended_t):
    token_rows = attended_t.shape[2]
    by_source = attended_t.transpose(2, 0, 1)
    returned = lax.all_to_all(by_source, "tok", split_axis=1, concat_axis=1, tiled=True)
    return returned.reshape(1, token_rows, -1)


def relocate_by_head(cache_blocks):
    tok_count = lax.axis_size("tok")
    local_blocks = cache_blocks[0]
    block_count, kv_count, heads_all, entries = local_blocks.shape
    split = local_blocks.reshape(block_count, kv_count, tok_count, heads_all // tok_count, entries)
    return lax.all_to_all(split, "tok", split_axis=2, concat_axis=2, tiled=True)


def place_slots(by_head, targets):
    groups = lax.axis_size("req")
    block_count = by_head.shape[0]
    positions = jnp.arange(block_count, dtype=jnp.int32)
    earlier = (targets[:, :, None] == targets[:, None, :]) & (positions[None, None, :] < positions[None, :, None])
    slot_rank = jnp.sum(earlier.astype(jnp.int32), axis=2)
    group_ids = jnp.arange(groups, dtype=jnp.int32)
    slot_ids = jnp.arange(CAP, dtype=jnp.int32)
    match = (
        (targets.T[None, None, :, :] == group_ids[:, None, None, None])
        & (slot_rank.T[None, None, :, :] == slot_ids[None, :, None, None])
    )
    picked = jnp.where(
        match[:, :, :, None, :, None, None], by_head[None, None], jnp.zeros((), by_head.dtype)
    )
    return jnp.sum(picked, axis=2, dtype=by_head.dtype)


def relocate_groups(outgoing):
    arrived = lax.all_to_all(outgoing, "req", split_axis=0, concat_axis=0, tiled=True)
    return arrived[None]


def on_device(query_rows, key_rows, value_rows, lengths, cache_blocks, destinations):
    span_length = query_rows.shape[1] * lax.axis_size("tok")
    segments = segment_ids(lengths[0], span_length)
    tok_count = lax.axis_size("tok")
    own_targets = destinations[0, :, 0]
    targets = lax.all_to_all(
        jnp.broadcast_to(own_targets[None, :], (tok_count, own_targets.shape[0])),
        "tok", split_axis=0, concat_axis=0, tiled=True,
    )
    query_split = query_rows[0].reshape(query_rows.shape[1], tok_count, -1)
    targets, query_split = lax.optimization_barrier((targets, query_split))
    query_t = lax.all_to_all(query_split, "tok", split_axis=1, concat_axis=1, tiled=True).transpose(1, 2, 0)
    by_head = relocate_by_head(cache_blocks)
    by_head, key_rows, value_rows = lax.optimization_barrier((by_head, key_rows, value_rows))
    outgoing = place_slots(by_head, targets)
    key_t, value_t = to_heads(key_rows), to_heads(value_rows)
    outgoing, query_t, key_t, value_t = lax.optimization_barrier((outgoing, query_t, key_t, value_t))
    moved_cache = relocate_groups(outgoing)
    attended_t = attend_local(query_t, key_t, value_t, lengths[0], segments)
    moved_cache, attended_t = lax.optimization_barrier((moved_cache, attended_t))
    attended = from_heads(attended_t)
    return (attended, moved_cache)


def solution(mesh):
    return jax.shard_map(
        on_device,
        mesh=mesh,
        in_specs=(
            P("req", "tok", None),
            P("req", "tok", None),
            P("req", "tok", None),
            P("req", None),
            P("req", "tok", None, None, None),
            P("req", "tok", None),
        ),
        out_specs=(P("req", "tok", None), P("req", None, None, None, None, "tok", None)),
        check_vma=False,
    )
```

```python
import functools

import jax
import jax.numpy as jnp
from jax import lax
from jax.experimental import pallas as pl
from jax.experimental.pallas import tpu as pltpu
from jax.sharding import PartitionSpec as P

HD = 224
CAP = 2
NEG = -1e30


def segment_ids(lengths_row, span_length):
    ends = jnp.cumsum(lengths_row)
    positions = jnp.arange(span_length, dtype=jnp.int32)
    return jnp.sum((positions[:, None] >= ends[None, :]).astype(jnp.int32), axis=1)


def attention_kernel(first_ref, seg_first_ref, seg_last_ref, q_ref, kv_ref, qseg_ref, kseg_ref, o_ref,
                     m_ref, l_ref, acc_ref, k_sc):
    qi = pl.program_id(0)
    chunks, _, width, rows = kv_ref.shape
    heads_here = width // HD
    nt = (((1,), (1,)), ((), ()))

    @pl.when(qi == 0)
    def _():
        eye = (
            lax.broadcasted_iota(jnp.int32, (rows, rows), 0) == lax.broadcasted_iota(jnp.int32, (rows, rows), 1)
        ).astype(jnp.bfloat16)

        def fill(c, carry):
            start = pl.multiple_of(c * rows, rows)
            for h in range(heads_here):
                k_sc[h, pl.ds(start, rows), :] = lax.dot_general(
                    eye, kv_ref[c, 0, h * HD:(h + 1) * HD, :], nt, preferred_element_type=jnp.float32
                ).astype(jnp.bfloat16)
            return carry

        lax.fori_loop(0, chunks, fill, 0)

    m_ref[...] = jnp.full(m_ref.shape, NEG, jnp.float32)
    l_ref[...] = jnp.zeros(l_ref.shape, jnp.float32)
    acc_ref[...] = jnp.zeros(acc_ref.shape, jnp.float32)
    scale = HD ** (-0.5)
    query_seg = qseg_ref[...]
    query_pos = qi * rows + lax.broadcasted_iota(jnp.int32, (1, rows), 1)

    def step(kb, masked):
        start = pl.multiple_of(kb * rows, rows)
        if masked:
            key_seg = kseg_ref[pl.ds(start, rows), :]
            key_pos = start + lax.broadcasted_iota(jnp.int32, (rows, 1), 0)
            visible = (key_seg == query_seg) & (key_pos <= query_pos)
        for h in range(heads_here):
            keys = k_sc[h, pl.ds(start, rows), :]
            scores = jnp.dot(keys, q_ref[0, h * HD:(h + 1) * HD, :], preferred_element_type=jnp.float32) * scale
            if masked:
                scores = jnp.where(visible, scores, NEG)
            m_old = m_ref[h]
            m_new = jnp.maximum(m_old, jnp.max(scores, axis=0, keepdims=True))
            alpha = jnp.exp(m_old - m_new)
            weights = jnp.exp(scores - m_new)
            if masked:
                weights = jnp.where(visible, weights, 0.0)
            l_ref[h] = alpha * l_ref[h] + jnp.sum(weights, axis=0, keepdims=True)
            m_ref[h] = m_new
            values = kv_ref[kb, 1, h * HD:(h + 1) * HD, :]
            acc_ref[h] = alpha * acc_ref[h] + jnp.dot(
                values, weights.astype(jnp.bfloat16), preferred_element_type=jnp.float32
            )

    def body(kb, carry):
        full = (kb < qi) & (seg_first_ref[kb] == seg_last_ref[qi])

        @pl.when(full)
        def _():
            step(kb, False)

        @pl.when(jnp.logical_not(full))
        def _():
            step(kb, True)

        return carry

    lax.fori_loop(first_ref[qi], qi + 1, body, 0)
    for h in range(heads_here):
        o_ref[0, h * HD:(h + 1) * HD, :] = (acc_ref[h] / l_ref[h]).astype(o_ref.dtype)


def attend_local(query_t, kv_t, lengths_row, segments):
    chunks, width, rows = query_t.shape
    heads_here = width // HD
    length = chunks * rows
    ends = jnp.cumsum(lengths_row)
    starts = ends - lengths_row
    seg_first = segments[::rows]
    seg_last = segments[rows - 1::rows]
    first_start = jnp.sum(
        jnp.where(seg_first[:, None] == jnp.arange(lengths_row.shape[0])[None, :], starts[None, :], 0), axis=1
    )
    first_chunk = (first_start // rows).astype(jnp.int32)
    qseg = segments.reshape(chunks, 1, rows)
    kseg = segments.reshape(length, 1)
    visible_pairs = length * length // 2
    cost = pl.CostEstimate(
        flops=int(4 * visible_pairs * width),
        transcendentals=int(heads_here * visible_pairs),
        bytes_accessed=int(4 * length * width * 2),
    )
    return pl.pallas_call(
        attention_kernel,
        out_shape=jax.ShapeDtypeStruct(query_t.shape, query_t.dtype),
        grid_spec=pltpu.PrefetchScalarGridSpec(
            num_scalar_prefetch=3,
            grid=(chunks,),
            in_specs=[
                pl.BlockSpec((1, width, rows), lambda i, *_: (i, 0, 0)),
                pl.BlockSpec((chunks, 2, width, rows), lambda i, *_: (0, 0, 0, 0), pipeline_mode=pl.Buffered(1)),
                pl.BlockSpec((None, 1, rows), lambda i, *_: (i, 0, 0)),
                pl.BlockSpec((length, 1), lambda i, *_: (0, 0), pipeline_mode=pl.Buffered(1)),
            ],
            out_specs=pl.BlockSpec((1, width, rows), lambda i, *_: (i, 0, 0)),
            scratch_shapes=[
                pltpu.VMEM((heads_here, 1, rows), jnp.float32),
                pltpu.VMEM((heads_here, 1, rows), jnp.float32),
                pltpu.VMEM((heads_here, HD, rows), jnp.float32),
                pltpu.VMEM((heads_here, length, HD), jnp.bfloat16),
            ],
        ),
        compiler_params=pltpu.CompilerParams(dimension_semantics=("arbitrary",)),
        cost_estimate=cost,
    )(first_chunk, seg_first, seg_last, query_t, kv_t, qseg, kseg)


def to_heads(rows_in):
    tok_count = lax.axis_size("tok")
    token_rows, feature_width = rows_in.shape[1], rows_in.shape[2]
    split = rows_in[0].reshape(token_rows, tok_count, feature_width // tok_count)
    gathered = lax.all_to_all(split, "tok", split_axis=1, concat_axis=1, tiled=True)
    return gathered.transpose(1, 2, 0)


def kv_to_heads(key_rows, value_rows):
    tok_count = lax.axis_size("tok")
    token_rows, feature_width = key_rows.shape[1], key_rows.shape[2]
    stacked = jnp.stack(
        [
            key_rows[0].reshape(token_rows, tok_count, feature_width // tok_count),
            value_rows[0].reshape(token_rows, tok_count, feature_width // tok_count),
        ],
        axis=2,
    )
    gathered = lax.all_to_all(stacked, "tok", split_axis=1, concat_axis=1, tiled=True)
    return gathered.transpose(1, 2, 3, 0)


def from_heads(attended_t):
    token_rows = attended_t.shape[2]
    by_source = attended_t.transpose(2, 0, 1)
    returned = lax.all_to_all(by_source, "tok", split_axis=1, concat_axis=1, tiled=True)
    return returned.reshape(1, token_rows, -1)


def relocate_by_head(cache_blocks):
    tok_count = lax.axis_size("tok")
    local_blocks = cache_blocks[0]
    block_count, kv_count, heads_all, entries = local_blocks.shape
    split = local_blocks.reshape(block_count, kv_count, tok_count, heads_all // tok_count, entries)
    return lax.all_to_all(split, "tok", split_axis=2, concat_axis=2, tiled=True)


def place_slots(by_head, targets):
    groups = lax.axis_size("req")
    block_count = by_head.shape[0]
    positions = jnp.arange(block_count, dtype=jnp.int32)
    earlier = (targets[:, :, None] == targets[:, None, :]) & (positions[None, None, :] < positions[None, :, None])
    slot_rank = jnp.sum(earlier.astype(jnp.int32), axis=2)
    group_ids = jnp.arange(groups, dtype=jnp.int32)
    slot_ids = jnp.arange(CAP, dtype=jnp.int32)
    match = (
        (targets.T[None, None, :, :] == group_ids[:, None, None, None])
        & (slot_rank.T[None, None, :, :] == slot_ids[None, :, None, None])
    )
    picked = jnp.where(
        match[:, :, :, None, :, None, None], by_head[None, None], jnp.zeros((), by_head.dtype)
    )
    return jnp.sum(picked, axis=2, dtype=by_head.dtype)


def relocate_groups(outgoing):
    arrived = lax.all_to_all(outgoing, "req", split_axis=0, concat_axis=0, tiled=True)
    return arrived[None]


def on_device(query_rows, key_rows, value_rows, lengths, cache_blocks, destinations):
    span_length = query_rows.shape[1] * lax.axis_size("tok")
    segments = segment_ids(lengths[0], span_length)
    tok_count = lax.axis_size("tok")
    own_targets = destinations[0, :, 0]
    targets = lax.all_to_all(
        jnp.broadcast_to(own_targets[None, :], (tok_count, own_targets.shape[0])),
        "tok", split_axis=0, concat_axis=0, tiled=True,
    )
    query_split = query_rows[0].reshape(query_rows.shape[1], tok_count, -1)
    targets, query_split = lax.optimization_barrier((targets, query_split))
    query_t = lax.all_to_all(query_split, "tok", split_axis=1, concat_axis=1, tiled=True).transpose(1, 2, 0)
    by_head = relocate_by_head(cache_blocks)
    by_head, key_rows, value_rows = lax.optimization_barrier((by_head, key_rows, value_rows))
    outgoing = place_slots(by_head, targets)
    kv_t = kv_to_heads(key_rows, value_rows)
    outgoing, query_t, kv_t = lax.optimization_barrier((outgoing, query_t, kv_t))
    moved_cache = relocate_groups(outgoing)
    attended_t = attend_local(query_t, kv_t, lengths[0], segments)
    moved_cache, attended_t = lax.optimization_barrier((moved_cache, attended_t))
    attended = from_heads(attended_t)
    return (attended, moved_cache)


def solution(mesh):
    return jax.shard_map(
        on_device,
        mesh=mesh,
        in_specs=(
            P("req", "tok", None),
            P("req", "tok", None),
            P("req", "tok", None),
            P("req", None),
            P("req", "tok", None, None, None),
            P("req", "tok", None),
        ),
        out_specs=(P("req", "tok", None), P("req", None, None, None, None, "tok", None)),
        check_vma=False,
    )
```

```python
import functools

import jax
import jax.numpy as jnp
from jax import lax
from jax.experimental import pallas as pl
from jax.experimental.pallas import tpu as pltpu
from jax.sharding import PartitionSpec as P

HD = 224
CAP = 2
NEG = -1e30


def segment_ids(lengths_row, span_length):
    ends = jnp.cumsum(lengths_row)
    positions = jnp.arange(span_length, dtype=jnp.int32)
    return jnp.sum((positions[:, None] >= ends[None, :]).astype(jnp.int32), axis=1)


def attention_kernel(first_ref, seg_first_ref, seg_last_ref, q_ref, kv_ref, qseg_ref, kseg_ref, o_ref,
                     m_ref, l_ref, acc_ref, k_sc):
    qi = pl.program_id(0)
    chunks, _, width, rows = kv_ref.shape
    heads_here = width // HD
    nt = (((1,), (1,)), ((), ()))

    @pl.when(qi == 0)
    def _():
        eye = (
            lax.broadcasted_iota(jnp.int32, (rows, rows), 0) == lax.broadcasted_iota(jnp.int32, (rows, rows), 1)
        ).astype(jnp.bfloat16)

        def fill(c, carry):
            start = pl.multiple_of(c * rows, rows)
            for h in range(heads_here):
                k_sc[h, pl.ds(start, rows), :] = lax.dot_general(
                    eye, kv_ref[c, 0, h * HD:(h + 1) * HD, :], nt, preferred_element_type=jnp.float32
                ).astype(jnp.bfloat16)
            return carry

        lax.fori_loop(0, chunks, fill, 0)

    m_ref[...] = jnp.full(m_ref.shape, NEG, jnp.float32)
    l_ref[...] = jnp.zeros(l_ref.shape, jnp.float32)
    acc_ref[...] = jnp.zeros(acc_ref.shape, jnp.float32)
    scale = HD ** (-0.5)
    query_seg = qseg_ref[...]
    query_pos = qi * rows + lax.broadcasted_iota(jnp.int32, (1, rows), 1)

    def step(kb, masked):
        start = pl.multiple_of(kb * rows, rows)
        if masked:
            key_seg = kseg_ref[pl.ds(start, rows), :]
            key_pos = start + lax.broadcasted_iota(jnp.int32, (rows, 1), 0)
            visible = (key_seg == query_seg) & (key_pos <= query_pos)
        for h in range(heads_here):
            keys = k_sc[h, pl.ds(start, rows), :]
            scores = jnp.dot(keys, q_ref[0, h * HD:(h + 1) * HD, :], preferred_element_type=jnp.float32) * scale
            if masked:
                scores = jnp.where(visible, scores, NEG)
            m_old = m_ref[h]
            m_new = jnp.maximum(m_old, jnp.max(scores, axis=0, keepdims=True))
            alpha = jnp.exp(m_old - m_new)
            weights = jnp.exp(scores - m_new)
            if masked:
                weights = jnp.where(visible, weights, 0.0)
            l_ref[h] = alpha * l_ref[h] + jnp.sum(weights, axis=0, keepdims=True)
            m_ref[h] = m_new
            values = kv_ref[kb, 1, h * HD:(h + 1) * HD, :]
            acc_ref[h] = alpha * acc_ref[h] + jnp.dot(
                values, weights.astype(jnp.bfloat16), preferred_element_type=jnp.float32
            )

    def body(kb, carry):
        full = (kb < qi) & (seg_first_ref[kb] == seg_last_ref[qi])

        @pl.when(full)
        def _():
            step(kb, False)

        @pl.when(jnp.logical_not(full))
        def _():
            step(kb, True)

        return carry

    lax.fori_loop(first_ref[qi], qi + 1, body, 0)
    for h in range(heads_here):
        o_ref[0, h * HD:(h + 1) * HD, :] = (acc_ref[h] / l_ref[h]).astype(o_ref.dtype)


def attend_local(qkv_t, lengths_row, segments):
    chunks, _, width, rows = qkv_t.shape
    heads_here = width // HD
    length = chunks * rows
    ends = jnp.cumsum(lengths_row)
    starts = ends - lengths_row
    seg_first = segments[::rows]
    seg_last = segments[rows - 1::rows]
    first_start = jnp.sum(
        jnp.where(seg_first[:, None] == jnp.arange(lengths_row.shape[0])[None, :], starts[None, :], 0), axis=1
    )
    first_chunk = (first_start // rows).astype(jnp.int32)
    qseg = segments.reshape(chunks, 1, rows)
    kseg = segments.reshape(length, 1)
    visible_pairs = length * length // 2
    cost = pl.CostEstimate(
        flops=int(4 * visible_pairs * width),
        transcendentals=int(heads_here * visible_pairs),
        bytes_accessed=int(4 * length * width * 2),
    )
    return pl.pallas_call(
        attention_kernel,
        out_shape=jax.ShapeDtypeStruct((chunks, width, rows), qkv_t.dtype),
        grid_spec=pltpu.PrefetchScalarGridSpec(
            num_scalar_prefetch=3,
            grid=(chunks,),
            in_specs=[
                pl.BlockSpec((1, None, width, rows), lambda i, *_: (i, 2, 0, 0)),
                pl.BlockSpec((chunks, 2, width, rows), lambda i, *_: (0, 0, 0, 0), pipeline_mode=pl.Buffered(1)),
                pl.BlockSpec((None, 1, rows), lambda i, *_: (i, 0, 0)),
                pl.BlockSpec((length, 1), lambda i, *_: (0, 0), pipeline_mode=pl.Buffered(1)),
            ],
            out_specs=pl.BlockSpec((1, width, rows), lambda i, *_: (i, 0, 0)),
            scratch_shapes=[
                pltpu.VMEM((heads_here, 1, rows), jnp.float32),
                pltpu.VMEM((heads_here, 1, rows), jnp.float32),
                pltpu.VMEM((heads_here, HD, rows), jnp.float32),
                pltpu.VMEM((heads_here, length, HD), jnp.bfloat16),
            ],
        ),
        compiler_params=pltpu.CompilerParams(dimension_semantics=("arbitrary",)),
        cost_estimate=cost,
    )(first_chunk, seg_first, seg_last, qkv_t, qkv_t, qseg, kseg)


def to_heads(rows_in):
    tok_count = lax.axis_size("tok")
    token_rows, feature_width = rows_in.shape[1], rows_in.shape[2]
    split = rows_in[0].reshape(token_rows, tok_count, feature_width // tok_count)
    gathered = lax.all_to_all(split, "tok", split_axis=1, concat_axis=1, tiled=True)
    return gathered.transpose(1, 2, 0)


def kv_to_heads(key_rows, value_rows, query_rows):
    tok_count = lax.axis_size("tok")
    token_rows, feature_width = key_rows.shape[1], key_rows.shape[2]
    stacked = jnp.stack(
        [
            rows_in[0].reshape(token_rows, tok_count, feature_width // tok_count)
            for rows_in in (key_rows, value_rows, query_rows)
        ],
        axis=2,
    )
    return stacked


def stacked_to_heads(stacked):
    gathered = lax.all_to_all(stacked, "tok", split_axis=1, concat_axis=1, tiled=True)
    return gathered.transpose(1, 2, 3, 0)


def from_heads(attended_t):
    token_rows = attended_t.shape[2]
    by_source = attended_t.transpose(2, 0, 1)
    returned = lax.all_to_all(by_source, "tok", split_axis=1, concat_axis=1, tiled=True)
    return returned.reshape(1, token_rows, -1)


def relocate_by_head(cache_blocks):
    tok_count = lax.axis_size("tok")
    local_blocks = cache_blocks[0]
    block_count, kv_count, heads_all, entries = local_blocks.shape
    split = local_blocks.reshape(block_count, kv_count, tok_count, heads_all // tok_count, entries)
    return lax.all_to_all(split, "tok", split_axis=2, concat_axis=2, tiled=True)


def place_slots(by_head, targets):
    groups = lax.axis_size("req")
    block_count = by_head.shape[0]
    positions = jnp.arange(block_count, dtype=jnp.int32)
    earlier = (targets[:, :, None] == targets[:, None, :]) & (positions[None, None, :] < positions[None, :, None])
    slot_rank = jnp.sum(earlier.astype(jnp.int32), axis=2)
    group_ids = jnp.arange(groups, dtype=jnp.int32)
    slot_ids = jnp.arange(CAP, dtype=jnp.int32)
    match = (
        (targets.T[None, None, :, :] == group_ids[:, None, None, None])
        & (slot_rank.T[None, None, :, :] == slot_ids[None, :, None, None])
    )
    picked = jnp.where(
        match[:, :, :, None, :, None, None], by_head[None, None], jnp.zeros((), by_head.dtype)
    )
    return jnp.sum(picked, axis=2, dtype=by_head.dtype)


def relocate_groups(outgoing):
    arrived = lax.all_to_all(outgoing, "req", split_axis=0, concat_axis=0, tiled=True)
    return arrived[None]


def on_device(query_rows, key_rows, value_rows, lengths, cache_blocks, destinations):
    span_length = query_rows.shape[1] * lax.axis_size("tok")
    segments = segment_ids(lengths[0], span_length)
    tok_count = lax.axis_size("tok")
    own_targets = destinations[0, :, 0]
    targets = lax.all_to_all(
        jnp.broadcast_to(own_targets[None, :], (tok_count, own_targets.shape[0])),
        "tok", split_axis=0, concat_axis=0, tiled=True,
    )
    by_head = relocate_by_head(cache_blocks)
    stacked = kv_to_heads(key_rows, value_rows, query_rows)
    by_head, stacked = lax.optimization_barrier((by_head, stacked))
    outgoing = place_slots(by_head, targets)
    qkv_t = stacked_to_heads(stacked)
    outgoing, qkv_t = lax.optimization_barrier((outgoing, qkv_t))
    moved_cache = relocate_groups(outgoing)
    attended_t = attend_local(qkv_t, lengths[0], segments)
    moved_cache, attended_t = lax.optimization_barrier((moved_cache, attended_t))
    attended = from_heads(attended_t)
    return (attended, moved_cache)


def solution(mesh):
    return jax.shard_map(
        on_device,
        mesh=mesh,
        in_specs=(
            P("req", "tok", None),
            P("req", "tok", None),
            P("req", "tok", None),
            P("req", None),
            P("req", "tok", None, None, None),
            P("req", "tok", None),
        ),
        out_specs=(P("req", "tok", None), P("req", None, None, None, None, "tok", None)),
        check_vma=False,
    )
```

```python
import functools

import jax
import jax.numpy as jnp
from jax import lax
from jax.experimental import pallas as pl
from jax.experimental.pallas import tpu as pltpu
from jax.sharding import PartitionSpec as P

HD = 224
CAP = 2
NEG = -1e30


def segment_ids(lengths_row, span_length):
    ends = jnp.cumsum(lengths_row)
    positions = jnp.arange(span_length, dtype=jnp.int32)
    return jnp.sum((positions[:, None] >= ends[None, :]).astype(jnp.int32), axis=1)


def attention_kernel(first_ref, seg_first_ref, seg_last_ref, q_ref, kv_ref, qseg_ref, kseg_ref, o_ref,
                     m_ref, l_ref, acc_ref, k_sc):
    qi = pl.program_id(0)
    chunks, _, width, rows = kv_ref.shape
    heads_here = width // HD
    nt = (((1,), (1,)), ((), ()))

    @pl.when(qi == 0)
    def _():
        eye = (
            lax.broadcasted_iota(jnp.int32, (rows, rows), 0) == lax.broadcasted_iota(jnp.int32, (rows, rows), 1)
        ).astype(jnp.bfloat16)

        def fill(c, carry):
            start = pl.multiple_of(c * rows, rows)
            for h in range(heads_here):
                k_sc[h, pl.ds(start, rows), :] = lax.dot_general(
                    eye, kv_ref[c, 0, h * HD:(h + 1) * HD, :], nt, preferred_element_type=jnp.float32
                ).astype(jnp.bfloat16)
            return carry

        lax.fori_loop(0, chunks, fill, 0)

    m_ref[...] = jnp.full(m_ref.shape, NEG, jnp.float32)
    l_ref[...] = jnp.zeros(l_ref.shape, jnp.float32)
    acc_ref[...] = jnp.zeros(acc_ref.shape, jnp.float32)
    scale = HD ** (-0.5)
    query_seg = qseg_ref[...]
    query_pos = qi * rows + lax.broadcasted_iota(jnp.int32, (1, rows), 1)

    def step(kb, masked):
        start = pl.multiple_of(kb * rows, rows)
        if masked:
            key_seg = kseg_ref[pl.ds(start, rows), :]
            key_pos = start + lax.broadcasted_iota(jnp.int32, (rows, 1), 0)
            visible = (key_seg == query_seg) & (key_pos <= query_pos)
        for h in range(heads_here):
            keys = k_sc[h, pl.ds(start, rows), :]
            scores = jnp.dot(keys, q_ref[0, h * HD:(h + 1) * HD, :], preferred_element_type=jnp.float32) * scale
            if masked:
                scores = jnp.where(visible, scores, NEG)
            m_old = m_ref[h]
            m_new = jnp.maximum(m_old, jnp.max(scores, axis=0, keepdims=True))
            alpha = jnp.exp(m_old - m_new)
            weights = jnp.exp(scores - m_new)
            if masked:
                weights = jnp.where(visible, weights, 0.0)
            l_ref[h] = alpha * l_ref[h] + jnp.sum(weights, axis=0, keepdims=True)
            m_ref[h] = m_new
            values = kv_ref[kb, 1, h * HD:(h + 1) * HD, :]
            acc_ref[h] = alpha * acc_ref[h] + jnp.dot(
                values, weights.astype(jnp.bfloat16), preferred_element_type=jnp.float32
            )

    def body(kb, carry):
        full = (kb < qi) & (seg_first_ref[kb] == seg_last_ref[qi])

        @pl.when(full)
        def _():
            step(kb, False)

        @pl.when(jnp.logical_not(full))
        def _():
            step(kb, True)

        return carry

    lax.fori_loop(first_ref[qi], qi + 1, body, 0)
    for h in range(heads_here):
        o_ref[0, h * HD:(h + 1) * HD, :] = (acc_ref[h] / l_ref[h]).astype(o_ref.dtype)


def attend_local(qkv_t, lengths_row, segments):
    chunks, _, width, rows = qkv_t.shape
    heads_here = width // HD
    length = chunks * rows
    ends = jnp.cumsum(lengths_row)
    starts = ends - lengths_row
    seg_first = segments[::rows]
    seg_last = segments[rows - 1::rows]
    first_start = jnp.sum(
        jnp.where(seg_first[:, None] == jnp.arange(lengths_row.shape[0])[None, :], starts[None, :], 0), axis=1
    )
    first_chunk = (first_start // rows).astype(jnp.int32)
    qseg = segments.reshape(chunks, 1, rows)
    kseg = segments.reshape(length, 1)
    visible_pairs = length * length // 2
    cost = pl.CostEstimate(
        flops=int(4 * visible_pairs * width),
        transcendentals=int(heads_here * visible_pairs),
        bytes_accessed=int(4 * length * width * 2),
    )
    return pl.pallas_call(
        attention_kernel,
        out_shape=jax.ShapeDtypeStruct((chunks, width, rows), qkv_t.dtype),
        grid_spec=pltpu.PrefetchScalarGridSpec(
            num_scalar_prefetch=3,
            grid=(chunks,),
            in_specs=[
                pl.BlockSpec((1, None, width, rows), lambda i, *_: (i, 2, 0, 0)),
                pl.BlockSpec((chunks, 2, width, rows), lambda i, *_: (0, 0, 0, 0), pipeline_mode=pl.Buffered(1)),
                pl.BlockSpec((None, 1, rows), lambda i, *_: (i, 0, 0)),
                pl.BlockSpec((length, 1), lambda i, *_: (0, 0), pipeline_mode=pl.Buffered(1)),
            ],
            out_specs=pl.BlockSpec((1, width, rows), lambda i, *_: (i, 0, 0)),
            scratch_shapes=[
                pltpu.VMEM((heads_here, 1, rows), jnp.float32),
                pltpu.VMEM((heads_here, 1, rows), jnp.float32),
                pltpu.VMEM((heads_here, HD, rows), jnp.float32),
                pltpu.VMEM((heads_here, length, HD), jnp.bfloat16),
            ],
        ),
        compiler_params=pltpu.CompilerParams(dimension_semantics=("arbitrary",)),
        cost_estimate=cost,
    )(first_chunk, seg_first, seg_last, qkv_t, qkv_t, qseg, kseg)


def to_heads(rows_in):
    tok_count = lax.axis_size("tok")
    token_rows, feature_width = rows_in.shape[1], rows_in.shape[2]
    split = rows_in[0].reshape(token_rows, tok_count, feature_width // tok_count)
    gathered = lax.all_to_all(split, "tok", split_axis=1, concat_axis=1, tiled=True)
    return gathered.transpose(1, 2, 0)


def kv_to_heads(key_rows, value_rows, query_rows):
    tok_count = lax.axis_size("tok")
    token_rows, feature_width = key_rows.shape[1], key_rows.shape[2]
    by_chunk = jnp.stack(
        [
            rows_in[0].reshape(token_rows, tok_count, feature_width // tok_count).transpose(1, 2, 0)
            for rows_in in (key_rows, value_rows, query_rows)
        ],
        axis=1,
    )
    return by_chunk.transpose(3, 0, 1, 2)


def stacked_to_heads(stacked):
    gathered = lax.all_to_all(stacked, "tok", split_axis=1, concat_axis=1, tiled=True)
    return gathered.transpose(1, 2, 3, 0)


def from_heads(attended_t):
    token_rows = attended_t.shape[2]
    by_source = attended_t.transpose(2, 0, 1)
    returned = lax.all_to_all(by_source, "tok", split_axis=1, concat_axis=1, tiled=True)
    return returned.reshape(1, token_rows, -1)


def relocate_by_head(cache_blocks):
    tok_count = lax.axis_size("tok")
    local_blocks = cache_blocks[0]
    block_count, kv_count, heads_all, entries = local_blocks.shape
    split = local_blocks.reshape(block_count, kv_count, tok_count, heads_all // tok_count, entries)
    return lax.all_to_all(split, "tok", split_axis=2, concat_axis=2, tiled=True)


def place_slots(by_head, targets):
    groups = lax.axis_size("req")
    block_count = by_head.shape[0]
    positions = jnp.arange(block_count, dtype=jnp.int32)
    earlier = (targets[:, :, None] == targets[:, None, :]) & (positions[None, None, :] < positions[None, :, None])
    slot_rank = jnp.sum(earlier.astype(jnp.int32), axis=2)
    group_ids = jnp.arange(groups, dtype=jnp.int32)
    slot_ids = jnp.arange(CAP, dtype=jnp.int32)
    match = (
        (targets.T[None, None, :, :] == group_ids[:, None, None, None])
        & (slot_rank.T[None, None, :, :] == slot_ids[None, :, None, None])
    )
    picked = jnp.where(
        match[:, :, :, None, :, None, None], by_head[None, None], jnp.zeros((), by_head.dtype)
    )
    return jnp.sum(picked, axis=2, dtype=by_head.dtype)


def relocate_groups(outgoing):
    arrived = lax.all_to_all(outgoing, "req", split_axis=0, concat_axis=0, tiled=True)
    return arrived[None]


def on_device(query_rows, key_rows, value_rows, lengths, cache_blocks, destinations):
    span_length = query_rows.shape[1] * lax.axis_size("tok")
    segments = segment_ids(lengths[0], span_length)
    tok_count = lax.axis_size("tok")
    own_targets = destinations[0, :, 0]
    targets = lax.all_to_all(
        jnp.broadcast_to(own_targets[None, :], (tok_count, own_targets.shape[0])),
        "tok", split_axis=0, concat_axis=0, tiled=True,
    )
    by_head = relocate_by_head(cache_blocks)
    stacked = kv_to_heads(key_rows, value_rows, query_rows)
    by_head, stacked = lax.optimization_barrier((by_head, stacked))
    outgoing = place_slots(by_head, targets)
    qkv_t = stacked_to_heads(stacked)
    outgoing, qkv_t = lax.optimization_barrier((outgoing, qkv_t))
    moved_cache = relocate_groups(outgoing)
    attended_t = attend_local(qkv_t, lengths[0], segments)
    moved_cache, attended_t = lax.optimization_barrier((moved_cache, attended_t))
    attended = from_heads(attended_t)
    return (attended, moved_cache)


def solution(mesh):
    return jax.shard_map(
        on_device,
        mesh=mesh,
        in_specs=(
            P("req", "tok", None),
            P("req", "tok", None),
            P("req", "tok", None),
            P("req", None),
            P("req", "tok", None, None, None),
            P("req", "tok", None),
        ),
        out_specs=(P("req", "tok", None), P("req", None, None, None, None, "tok", None)),
        check_vma=False,
    )
```

```python
import functools

import jax
import jax.numpy as jnp
from jax import lax
from jax.experimental import pallas as pl
from jax.experimental.pallas import tpu as pltpu
from jax.sharding import PartitionSpec as P

HD = 224
CAP = 2
NEG = -1e30


def segment_ids(lengths_row, span_length):
    ends = jnp.cumsum(lengths_row)
    positions = jnp.arange(span_length, dtype=jnp.int32)
    return jnp.sum((positions[:, None] >= ends[None, :]).astype(jnp.int32), axis=1)


def attention_kernel(first_ref, seg_first_ref, seg_last_ref, q_ref, kv_ref, qseg_ref, kseg_ref, o_ref,
                     m_ref, l_ref, acc_ref, k_sc):
    qi = pl.program_id(0)
    chunks, _, width, rows = kv_ref.shape
    heads_here = width // HD
    nt = (((1,), (1,)), ((), ()))

    @pl.when(qi == 0)
    def _():
        eye = (
            lax.broadcasted_iota(jnp.int32, (rows, rows), 0) == lax.broadcasted_iota(jnp.int32, (rows, rows), 1)
        ).astype(jnp.bfloat16)

        def fill(c, carry):
            start = pl.multiple_of(c * rows, rows)
            for h in range(heads_here):
                k_sc[h, pl.ds(start, rows), :] = lax.dot_general(
                    eye, kv_ref[c, 0, h * HD:(h + 1) * HD, :], nt, preferred_element_type=jnp.float32
                ).astype(jnp.bfloat16)
            return carry

        lax.fori_loop(0, chunks, fill, 0)

    m_ref[...] = jnp.full(m_ref.shape, NEG, jnp.float32)
    l_ref[...] = jnp.zeros(l_ref.shape, jnp.float32)
    acc_ref[...] = jnp.zeros(acc_ref.shape, jnp.float32)
    scale = HD ** (-0.5)
    query_seg = qseg_ref[...]
    query_pos = qi * rows + lax.broadcasted_iota(jnp.int32, (1, rows), 1)

    def step(kb, masked):
        start = pl.multiple_of(kb * rows, rows)
        if masked:
            key_seg = kseg_ref[pl.ds(start, rows), :]
            key_pos = start + lax.broadcasted_iota(jnp.int32, (rows, 1), 0)
            visible = (key_seg == query_seg) & (key_pos <= query_pos)
        for h in range(heads_here):
            keys = k_sc[h, pl.ds(start, rows), :]
            scores = jnp.dot(keys, q_ref[0, h * HD:(h + 1) * HD, :], preferred_element_type=jnp.float32) * scale
            if masked:
                scores = jnp.where(visible, scores, NEG)
            m_old = m_ref[h]
            m_new = jnp.maximum(m_old, jnp.max(scores, axis=0, keepdims=True))
            alpha = jnp.exp(m_old - m_new)
            weights = jnp.exp(scores - m_new)
            if masked:
                weights = jnp.where(visible, weights, 0.0)
            l_ref[h] = alpha * l_ref[h] + jnp.sum(weights, axis=0, keepdims=True)
            m_ref[h] = m_new
            values = kv_ref[kb, 1, h * HD:(h + 1) * HD, :]
            acc_ref[h] = alpha * acc_ref[h] + jnp.dot(
                values, weights.astype(jnp.bfloat16), preferred_element_type=jnp.float32
            )

    def body(kb, carry):
        full = (kb < qi) & (seg_first_ref[kb] == seg_last_ref[qi])

        @pl.when(full)
        def _():
            step(kb, False)

        @pl.when(jnp.logical_not(full))
        def _():
            step(kb, True)

        return carry

    lax.fori_loop(first_ref[qi], qi + 1, body, 0)
    for h in range(heads_here):
        o_ref[0, h * HD:(h + 1) * HD, :] = (acc_ref[h] / l_ref[h]).astype(o_ref.dtype)


def attend_local(qkv_t, lengths_row, segments):
    chunks, _, width, rows = qkv_t.shape
    heads_here = width // HD
    length = chunks * rows
    ends = jnp.cumsum(lengths_row)
    starts = ends - lengths_row
    seg_first = segments[::rows]
    seg_last = segments[rows - 1::rows]
    first_start = jnp.sum(
        jnp.where(seg_first[:, None] == jnp.arange(lengths_row.shape[0])[None, :], starts[None, :], 0), axis=1
    )
    first_chunk = (first_start // rows).astype(jnp.int32)
    qseg = segments.reshape(chunks, 1, rows)
    kseg = segments.reshape(length, 1)
    visible_pairs = length * length // 2
    cost = pl.CostEstimate(
        flops=int(4 * visible_pairs * width),
        transcendentals=int(heads_here * visible_pairs),
        bytes_accessed=int(4 * length * width * 2),
    )
    return pl.pallas_call(
        attention_kernel,
        out_shape=jax.ShapeDtypeStruct((chunks, width, rows), qkv_t.dtype),
        grid_spec=pltpu.PrefetchScalarGridSpec(
            num_scalar_prefetch=3,
            grid=(chunks,),
            in_specs=[
                pl.BlockSpec((1, None, width, rows), lambda i, *_: (i, 2, 0, 0)),
                pl.BlockSpec((chunks, 2, width, rows), lambda i, *_: (0, 0, 0, 0), pipeline_mode=pl.Buffered(1)),
                pl.BlockSpec((None, 1, rows), lambda i, *_: (i, 0, 0)),
                pl.BlockSpec((length, 1), lambda i, *_: (0, 0), pipeline_mode=pl.Buffered(1)),
            ],
            out_specs=pl.BlockSpec((1, width, rows), lambda i, *_: (i, 0, 0)),
            scratch_shapes=[
                pltpu.VMEM((heads_here, 1, rows), jnp.float32),
                pltpu.VMEM((heads_here, 1, rows), jnp.float32),
                pltpu.VMEM((heads_here, HD, rows), jnp.float32),
                pltpu.VMEM((heads_here, length, HD), jnp.bfloat16),
            ],
        ),
        compiler_params=pltpu.CompilerParams(dimension_semantics=("arbitrary",)),
        cost_estimate=cost,
    )(first_chunk, seg_first, seg_last, qkv_t, qkv_t, qseg, kseg)


def to_heads(rows_in):
    tok_count = lax.axis_size("tok")
    token_rows, feature_width = rows_in.shape[1], rows_in.shape[2]
    split = rows_in[0].reshape(token_rows, tok_count, feature_width // tok_count)
    gathered = lax.all_to_all(split, "tok", split_axis=1, concat_axis=1, tiled=True)
    return gathered.transpose(1, 2, 0)


def kv_to_heads(key_rows, value_rows, query_rows):
    tok_count = lax.axis_size("tok")
    token_rows, feature_width = key_rows.shape[1], key_rows.shape[2]
    by_chunk = jnp.stack(
        [
            rows_in[0].reshape(token_rows, tok_count, feature_width // tok_count).transpose(1, 2, 0)
            for rows_in in (key_rows, value_rows, query_rows)
        ],
        axis=1,
    )
    return by_chunk.transpose(3, 0, 1, 2)


def stacked_to_heads(stacked):
    gathered = lax.all_to_all(stacked, "tok", split_axis=1, concat_axis=1, tiled=True)
    return gathered.transpose(1, 2, 3, 0)


def from_heads(attended_t):
    token_rows = attended_t.shape[2]
    by_source = attended_t.transpose(2, 0, 1)
    returned = lax.all_to_all(by_source, "tok", split_axis=1, concat_axis=1, tiled=True)
    return returned.reshape(1, token_rows, -1)


def relocate_by_head(cache_blocks):
    tok_count = lax.axis_size("tok")
    local_blocks = cache_blocks[0]
    block_count, kv_count, heads_all, entries = local_blocks.shape
    split = local_blocks.reshape(block_count, kv_count, tok_count, heads_all // tok_count, entries)
    return lax.all_to_all(split, "tok", split_axis=2, concat_axis=2, tiled=True)


def place_slots(by_head, targets):
    groups = lax.axis_size("req")
    block_count = by_head.shape[0]
    positions = jnp.arange(block_count, dtype=jnp.int32)
    earlier = (targets[:, :, None] == targets[:, None, :]) & (positions[None, None, :] < positions[None, :, None])
    slot_rank = jnp.sum(earlier.astype(jnp.int32), axis=2)
    group_ids = jnp.arange(groups, dtype=jnp.int32)
    slot_ids = jnp.arange(CAP, dtype=jnp.int32)
    match = (
        (targets.T[None, None, :, :] == group_ids[:, None, None, None])
        & (slot_rank.T[None, None, :, :] == slot_ids[None, :, None, None])
    )
    picked = jnp.where(
        match[:, :, :, None, :, None, None], by_head[None, None], jnp.zeros((), by_head.dtype)
    )
    return jnp.sum(picked, axis=2, dtype=by_head.dtype)


def relocate_groups(outgoing):
    arrived = lax.all_to_all(outgoing, "req", split_axis=0, concat_axis=0, tiled=True)
    return arrived[None]


def on_device(query_rows, key_rows, value_rows, lengths, cache_blocks, destinations):
    span_length = query_rows.shape[1] * lax.axis_size("tok")
    segments = segment_ids(lengths[0], span_length)
    tok_count = lax.axis_size("tok")
    by_head = relocate_by_head(cache_blocks)
    stacked = kv_to_heads(key_rows, value_rows, query_rows)
    stacked, destinations = lax.optimization_barrier((stacked, destinations))
    own_targets = destinations[0, :, 0]
    targets = lax.all_to_all(
        jnp.broadcast_to(own_targets[None, :], (tok_count, own_targets.shape[0])),
        "tok", split_axis=0, concat_axis=0, tiled=True,
    )
    by_head, stacked = lax.optimization_barrier((by_head, stacked))
    outgoing = place_slots(by_head, targets)
    qkv_t = stacked_to_heads(stacked)
    outgoing, qkv_t = lax.optimization_barrier((outgoing, qkv_t))
    moved_cache = relocate_groups(outgoing)
    attended_t = attend_local(qkv_t, lengths[0], segments)
    moved_cache, attended_t = lax.optimization_barrier((moved_cache, attended_t))
    attended = from_heads(attended_t)
    return (attended, moved_cache)


def solution(mesh):
    return jax.shard_map(
        on_device,
        mesh=mesh,
        in_specs=(
            P("req", "tok", None),
            P("req", "tok", None),
            P("req", "tok", None),
            P("req", None),
            P("req", "tok", None, None, None),
            P("req", "tok", None),
        ),
        out_specs=(P("req", "tok", None), P("req", None, None, None, None, "tok", None)),
        check_vma=False,
    )
```

```python
import functools

import jax
import jax.numpy as jnp
from jax import lax
from jax.experimental import pallas as pl
from jax.experimental.pallas import tpu as pltpu
from jax.sharding import PartitionSpec as P

HD = 224
CAP = 2
NEG = -1e30


def segment_ids(lengths_row, span_length):
    ends = jnp.cumsum(lengths_row)
    positions = jnp.arange(span_length, dtype=jnp.int32)
    return jnp.sum((positions[:, None] >= ends[None, :]).astype(jnp.int32), axis=1)


def attention_kernel(first_ref, seg_first_ref, seg_last_ref, q_ref, kv_ref, qseg_ref, kseg_ref, o_ref,
                     m_ref, l_ref, acc_ref, k_sc):
    qi = pl.program_id(0)
    chunks, _, width, rows = kv_ref.shape
    heads_here = width // HD
    nt = (((1,), (1,)), ((), ()))

    @pl.when(qi == 0)
    def _():
        eye = (
            lax.broadcasted_iota(jnp.int32, (rows, rows), 0) == lax.broadcasted_iota(jnp.int32, (rows, rows), 1)
        ).astype(jnp.bfloat16)

        def fill(c, carry):
            start = pl.multiple_of(c * rows, rows)
            for h in range(heads_here):
                k_sc[h, pl.ds(start, rows), :] = lax.dot_general(
                    eye, kv_ref[c, 0, h * HD:(h + 1) * HD, :], nt, preferred_element_type=jnp.float32
                ).astype(jnp.bfloat16)
            return carry

        lax.fori_loop(0, chunks, fill, 0)

    m_ref[...] = jnp.full(m_ref.shape, NEG, jnp.float32)
    l_ref[...] = jnp.zeros(l_ref.shape, jnp.float32)
    acc_ref[...] = jnp.zeros(acc_ref.shape, jnp.float32)
    scale = HD ** (-0.5)
    query_seg = qseg_ref[...]
    query_pos = qi * rows + lax.broadcasted_iota(jnp.int32, (1, rows), 1)

    def step(kb, masked):
        start = pl.multiple_of(kb * rows, rows)
        if masked:
            key_seg = kseg_ref[pl.ds(start, rows), :]
            key_pos = start + lax.broadcasted_iota(jnp.int32, (rows, 1), 0)
            visible = (key_seg == query_seg) & (key_pos <= query_pos)
        for h in range(heads_here):
            keys = k_sc[h, pl.ds(start, rows), :]
            scores = jnp.dot(keys, q_ref[0, h * HD:(h + 1) * HD, :], preferred_element_type=jnp.float32) * scale
            if masked:
                scores = jnp.where(visible, scores, NEG)
            m_old = m_ref[h]
            m_new = jnp.maximum(m_old, jnp.max(scores, axis=0, keepdims=True))
            alpha = jnp.exp(m_old - m_new)
            weights = jnp.exp(scores - m_new)
            if masked:
                weights = jnp.where(visible, weights, 0.0)
            l_ref[h] = alpha * l_ref[h] + jnp.sum(weights, axis=0, keepdims=True)
            m_ref[h] = m_new
            values = kv_ref[kb, 1, h * HD:(h + 1) * HD, :]
            acc_ref[h] = alpha * acc_ref[h] + jnp.dot(
                values, weights.astype(jnp.bfloat16), preferred_element_type=jnp.float32
            )

    def body(kb, carry):
        full = (kb < qi) & (seg_first_ref[kb] == seg_last_ref[qi])

        @pl.when(full)
        def _():
            step(kb, False)

        @pl.when(jnp.logical_not(full))
        def _():
            step(kb, True)

        return carry

    lax.fori_loop(first_ref[qi], qi + 1, body, 0)
    for h in range(heads_here):
        o_ref[0, h * HD:(h + 1) * HD, :] = (acc_ref[h] / l_ref[h]).astype(o_ref.dtype)


def attend_local(qkv_t, lengths_row, segments):
    chunks, _, width, rows = qkv_t.shape
    heads_here = width // HD
    length = chunks * rows
    ends = jnp.cumsum(lengths_row)
    starts = ends - lengths_row
    seg_first = segments[::rows]
    seg_last = segments[rows - 1::rows]
    first_start = jnp.sum(
        jnp.where(seg_first[:, None] == jnp.arange(lengths_row.shape[0])[None, :], starts[None, :], 0), axis=1
    )
    first_chunk = (first_start // rows).astype(jnp.int32)
    qseg = segments.reshape(chunks, 1, rows)
    kseg = segments.reshape(length, 1)
    visible_pairs = length * length // 2
    cost = pl.CostEstimate(
        flops=int(4 * visible_pairs * width),
        transcendentals=int(heads_here * visible_pairs),
        bytes_accessed=int(4 * length * width * 2),
    )
    return pl.pallas_call(
        attention_kernel,
        out_shape=jax.ShapeDtypeStruct((chunks, width, rows), qkv_t.dtype),
        grid_spec=pltpu.PrefetchScalarGridSpec(
            num_scalar_prefetch=3,
            grid=(chunks,),
            in_specs=[
                pl.BlockSpec((1, None, width, rows), lambda i, *_: (i, 2, 0, 0)),
                pl.BlockSpec((chunks, 2, width, rows), lambda i, *_: (0, 0, 0, 0), pipeline_mode=pl.Buffered(1)),
                pl.BlockSpec((None, 1, rows), lambda i, *_: (i, 0, 0)),
                pl.BlockSpec((length, 1), lambda i, *_: (0, 0), pipeline_mode=pl.Buffered(1)),
            ],
            out_specs=pl.BlockSpec((1, width, rows), lambda i, *_: (i, 0, 0)),
            scratch_shapes=[
                pltpu.VMEM((heads_here, 1, rows), jnp.float32),
                pltpu.VMEM((heads_here, 1, rows), jnp.float32),
                pltpu.VMEM((heads_here, HD, rows), jnp.float32),
                pltpu.VMEM((heads_here, length, HD), jnp.bfloat16),
            ],
        ),
        compiler_params=pltpu.CompilerParams(dimension_semantics=("arbitrary",)),
        cost_estimate=cost,
    )(first_chunk, seg_first, seg_last, qkv_t, qkv_t, qseg, kseg)


def to_heads(rows_in):
    tok_count = lax.axis_size("tok")
    token_rows, feature_width = rows_in.shape[1], rows_in.shape[2]
    split = rows_in[0].reshape(token_rows, tok_count, feature_width // tok_count)
    gathered = lax.all_to_all(split, "tok", split_axis=1, concat_axis=1, tiled=True)
    return gathered.transpose(1, 2, 0)


def kv_to_heads(key_rows, value_rows, query_rows):
    tok_count = lax.axis_size("tok")
    token_rows, feature_width = key_rows.shape[1], key_rows.shape[2]
    by_chunk = jnp.stack(
        [
            rows_in[0].reshape(token_rows, tok_count, feature_width // tok_count).transpose(1, 2, 0)
            for rows_in in (key_rows, value_rows, query_rows)
        ],
        axis=1,
    )
    return by_chunk.transpose(3, 0, 1, 2)


def stacked_to_heads(stacked):
    gathered = lax.all_to_all(stacked, "tok", split_axis=1, concat_axis=1, tiled=True)
    return gathered.transpose(1, 2, 3, 0)


def from_heads(attended_t):
    token_rows = attended_t.shape[2]
    by_source = attended_t.transpose(2, 0, 1)
    returned = lax.all_to_all(by_source, "tok", split_axis=1, concat_axis=1, tiled=True)
    return returned.reshape(1, token_rows, -1)


def relocate_by_head(cache_blocks):
    tok_count = lax.axis_size("tok")
    local_blocks = cache_blocks[0]
    block_count, kv_count, heads_all, entries = local_blocks.shape
    split = local_blocks.reshape(block_count, kv_count, tok_count, heads_all // tok_count, entries)
    return lax.all_to_all(split, "tok", split_axis=2, concat_axis=2, tiled=True)


def place_slots(by_head, targets):
    groups = lax.axis_size("req")
    block_count = by_head.shape[0]
    positions = jnp.arange(block_count, dtype=jnp.int32)
    earlier = (targets[:, :, None] == targets[:, None, :]) & (positions[None, None, :] < positions[None, :, None])
    slot_rank = jnp.sum(earlier.astype(jnp.int32), axis=2)
    group_ids = jnp.arange(groups, dtype=jnp.int32)
    slot_ids = jnp.arange(CAP, dtype=jnp.int32)
    match = (
        (targets.T[None, None, :, :] == group_ids[:, None, None, None])
        & (slot_rank.T[None, None, :, :] == slot_ids[None, :, None, None])
    )
    picked = jnp.where(
        match[:, :, :, None, :, None, None], by_head[None, None], jnp.zeros((), by_head.dtype)
    )
    return jnp.sum(picked, axis=2, dtype=by_head.dtype)


def relocate_groups(outgoing):
    arrived = lax.all_to_all(outgoing, "req", split_axis=0, concat_axis=0, tiled=True)
    return arrived[None]


def on_device(query_rows, key_rows, value_rows, lengths, cache_blocks, destinations):
    span_length = query_rows.shape[1] * lax.axis_size("tok")
    segments = segment_ids(lengths[0], span_length)
    tok_count = lax.axis_size("tok")
    own_targets = destinations[0, :, 0]
    targets = lax.all_to_all(
        jnp.broadcast_to(own_targets[None, :], (tok_count, own_targets.shape[0])),
        "tok", split_axis=0, concat_axis=0, tiled=True,
    )
    targets, cache_blocks = lax.optimization_barrier((targets, cache_blocks))
    by_head = relocate_by_head(cache_blocks)
    stacked = kv_to_heads(key_rows, value_rows, query_rows)
    by_head, stacked = lax.optimization_barrier((by_head, stacked))
    outgoing = place_slots(by_head, targets)
    qkv_t = stacked_to_heads(stacked)
    outgoing, qkv_t = lax.optimization_barrier((outgoing, qkv_t))
    moved_cache = relocate_groups(outgoing)
    attended_t = attend_local(qkv_t, lengths[0], segments)
    moved_cache, attended_t = lax.optimization_barrier((moved_cache, attended_t))
    attended = from_heads(attended_t)
    return (attended, moved_cache)


def solution(mesh):
    return jax.shard_map(
        on_device,
        mesh=mesh,
        in_specs=(
            P("req", "tok", None),
            P("req", "tok", None),
            P("req", "tok", None),
            P("req", None),
            P("req", "tok", None, None, None),
            P("req", "tok", None),
        ),
        out_specs=(P("req", "tok", None), P("req", None, None, None, None, "tok", None)),
        check_vma=False,
    )
```

```python
import functools

import jax
import jax.numpy as jnp
from jax import lax
from jax.experimental import pallas as pl
from jax.experimental.pallas import tpu as pltpu
from jax.sharding import PartitionSpec as P

HD = 224
CAP = 2
NEG = -1e30


def segment_ids(lengths_row, span_length):
    ends = jnp.cumsum(lengths_row)
    positions = jnp.arange(span_length, dtype=jnp.int32)
    return jnp.sum((positions[:, None] >= ends[None, :]).astype(jnp.int32), axis=1)


def attention_kernel(first_ref, seg_first_ref, seg_last_ref, q_ref, kv_ref, qseg_ref, kseg_ref, o_ref,
                     m_ref, l_ref, acc_ref, k_sc):
    qi = pl.program_id(0)
    chunks, _, width, rows = kv_ref.shape
    heads_here = width // HD
    nt = (((1,), (1,)), ((), ()))

    @pl.when(qi == 0)
    def _():
        eye = (
            lax.broadcasted_iota(jnp.int32, (rows, rows), 0) == lax.broadcasted_iota(jnp.int32, (rows, rows), 1)
        ).astype(jnp.bfloat16)

        def fill(c, carry):
            start = pl.multiple_of(c * rows, rows)
            for h in range(heads_here):
                k_sc[h, pl.ds(start, rows), :] = lax.dot_general(
                    eye, kv_ref[c, 0, h * HD:(h + 1) * HD, :], nt, preferred_element_type=jnp.float32
                ).astype(jnp.bfloat16)
            return carry

        lax.fori_loop(0, chunks, fill, 0)

    m_ref[...] = jnp.full(m_ref.shape, NEG, jnp.float32)
    l_ref[...] = jnp.zeros(l_ref.shape, jnp.float32)
    acc_ref[...] = jnp.zeros(acc_ref.shape, jnp.float32)
    scale = HD ** (-0.5)
    query_seg = qseg_ref[...]
    query_pos = qi * rows + lax.broadcasted_iota(jnp.int32, (1, rows), 1)

    def step(kb, masked):
        start = pl.multiple_of(kb * rows, rows)
        if masked:
            key_seg = kseg_ref[pl.ds(start, rows), :]
            key_pos = start + lax.broadcasted_iota(jnp.int32, (rows, 1), 0)
            visible = (key_seg == query_seg) & (key_pos <= query_pos)
        for h in range(heads_here):
            keys = k_sc[h, pl.ds(start, rows), :]
            scores = jnp.dot(keys, q_ref[0, h * HD:(h + 1) * HD, :], preferred_element_type=jnp.float32) * scale
            if masked:
                scores = jnp.where(visible, scores, NEG)
            m_old = m_ref[h]
            m_new = jnp.maximum(m_old, jnp.max(scores, axis=0, keepdims=True))
            alpha = jnp.exp(m_old - m_new)
            weights = jnp.exp(scores - m_new)
            if masked:
                weights = jnp.where(visible, weights, 0.0)
            l_ref[h] = alpha * l_ref[h] + jnp.sum(weights, axis=0, keepdims=True)
            m_ref[h] = m_new
            values = kv_ref[kb, 1, h * HD:(h + 1) * HD, :]
            acc_ref[h] = alpha * acc_ref[h] + jnp.dot(
                values, weights.astype(jnp.bfloat16), preferred_element_type=jnp.float32
            )

    def body(kb, carry):
        full = (kb < qi) & (seg_first_ref[kb] == seg_last_ref[qi])

        @pl.when(full)
        def _():
            step(kb, False)

        @pl.when(jnp.logical_not(full))
        def _():
            step(kb, True)

        return carry

    lax.fori_loop(first_ref[qi], qi + 1, body, 0)
    for h in range(heads_here):
        o_ref[0, h * HD:(h + 1) * HD, :] = (acc_ref[h] / l_ref[h]).astype(o_ref.dtype)


def attend_local(qkv_t, lengths_row, segments):
    chunks, _, width, rows = qkv_t.shape
    heads_here = width // HD
    length = chunks * rows
    ends = jnp.cumsum(lengths_row)
    starts = ends - lengths_row
    seg_first = segments[::rows]
    seg_last = segments[rows - 1::rows]
    first_start = jnp.sum(
        jnp.where(seg_first[:, None] == jnp.arange(lengths_row.shape[0])[None, :], starts[None, :], 0), axis=1
    )
    first_chunk = (first_start // rows).astype(jnp.int32)
    qseg = segments.reshape(chunks, 1, rows)
    kseg = segments.reshape(length, 1)
    visible_pairs = length * length // 2
    cost = pl.CostEstimate(
        flops=int(4 * visible_pairs * width),
        transcendentals=int(heads_here * visible_pairs),
        bytes_accessed=int(4 * length * width * 2),
    )
    return pl.pallas_call(
        attention_kernel,
        out_shape=jax.ShapeDtypeStruct((chunks, width, rows), qkv_t.dtype),
        grid_spec=pltpu.PrefetchScalarGridSpec(
            num_scalar_prefetch=3,
            grid=(chunks,),
            in_specs=[
                pl.BlockSpec((1, None, width, rows), lambda i, *_: (i, 2, 0, 0)),
                pl.BlockSpec((chunks, 2, width, rows), lambda i, *_: (0, 0, 0, 0), pipeline_mode=pl.Buffered(1)),
                pl.BlockSpec((None, 1, rows), lambda i, *_: (i, 0, 0)),
                pl.BlockSpec((length, 1), lambda i, *_: (0, 0), pipeline_mode=pl.Buffered(1)),
            ],
            out_specs=pl.BlockSpec((1, width, rows), lambda i, *_: (i, 0, 0)),
            scratch_shapes=[
                pltpu.VMEM((heads_here, 1, rows), jnp.float32),
                pltpu.VMEM((heads_here, 1, rows), jnp.float32),
                pltpu.VMEM((heads_here, HD, rows), jnp.float32),
                pltpu.VMEM((heads_here, length, HD), jnp.bfloat16),
            ],
        ),
        compiler_params=pltpu.CompilerParams(dimension_semantics=("arbitrary",)),
        cost_estimate=cost,
    )(first_chunk, seg_first, seg_last, qkv_t, qkv_t, qseg, kseg)


def to_heads(rows_in):
    tok_count = lax.axis_size("tok")
    token_rows, feature_width = rows_in.shape[1], rows_in.shape[2]
    split = rows_in[0].reshape(token_rows, tok_count, feature_width // tok_count)
    gathered = lax.all_to_all(split, "tok", split_axis=1, concat_axis=1, tiled=True)
    return gathered.transpose(1, 2, 0)


def kv_to_heads(key_rows, value_rows, query_rows):
    tok_count = lax.axis_size("tok")
    token_rows, feature_width = key_rows.shape[1], key_rows.shape[2]
    by_chunk = jnp.stack(
        [
            rows_in[0].reshape(token_rows, tok_count, feature_width // tok_count).transpose(1, 2, 0)
            for rows_in in (key_rows, value_rows, query_rows)
        ],
        axis=1,
    )
    return by_chunk.transpose(3, 0, 1, 2)


def stacked_to_heads(stacked):
    gathered = lax.all_to_all(stacked, "tok", split_axis=1, concat_axis=1, tiled=True)
    return gathered.transpose(1, 2, 3, 0)


def from_heads(attended_t):
    token_rows = attended_t.shape[2]
    by_source = attended_t.transpose(2, 0, 1)
    returned = lax.all_to_all(by_source, "tok", split_axis=1, concat_axis=1, tiled=True)
    return returned.reshape(1, token_rows, -1)


def relocate_by_head(cache_blocks):
    tok_count = lax.axis_size("tok")
    local_blocks = cache_blocks[0]
    block_count, kv_count, heads_all, entries = local_blocks.shape
    split = local_blocks.reshape(block_count, kv_count, tok_count, heads_all // tok_count, entries)
    return lax.all_to_all(split, "tok", split_axis=2, concat_axis=2, tiled=True)


def place_slots(by_head, targets):
    groups = lax.axis_size("req")
    block_count = by_head.shape[0]
    positions = jnp.arange(block_count, dtype=jnp.int32)
    earlier = (targets[:, :, None] == targets[:, None, :]) & (positions[None, None, :] < positions[None, :, None])
    slot_rank = jnp.sum(earlier.astype(jnp.int32), axis=2)
    group_ids = jnp.arange(groups, dtype=jnp.int32)
    slot_ids = jnp.arange(CAP, dtype=jnp.int32)
    match = (
        (targets.T[None, None, :, :] == group_ids[:, None, None, None])
        & (slot_rank.T[None, None, :, :] == slot_ids[None, :, None, None])
    )
    picked = jnp.where(
        match[:, :, :, None, :, None, None], by_head[None, None], jnp.zeros((), by_head.dtype)
    )
    return jnp.sum(picked, axis=2, dtype=by_head.dtype)


def relocate_groups(outgoing):
    arrived = lax.all_to_all(outgoing, "req", split_axis=0, concat_axis=0, tiled=True)
    return arrived[None]


def on_device(query_rows, key_rows, value_rows, lengths, cache_blocks, destinations):
    span_length = query_rows.shape[1] * lax.axis_size("tok")
    segments = segment_ids(lengths[0], span_length)
    tok_count = lax.axis_size("tok")
    own_targets = destinations[0, :, 0]
    targets = lax.all_to_all(
        jnp.broadcast_to(own_targets[None, :], (tok_count, own_targets.shape[0])),
        "tok", split_axis=0, concat_axis=0, tiled=True,
    )
    targets, key_rows, value_rows, query_rows = lax.optimization_barrier((targets, key_rows, value_rows, query_rows))
    by_head = relocate_by_head(cache_blocks)
    stacked = kv_to_heads(key_rows, value_rows, query_rows)
    by_head, stacked = lax.optimization_barrier((by_head, stacked))
    outgoing = place_slots(by_head, targets)
    qkv_t = stacked_to_heads(stacked)
    outgoing, qkv_t = lax.optimization_barrier((outgoing, qkv_t))
    moved_cache = relocate_groups(outgoing)
    attended_t = attend_local(qkv_t, lengths[0], segments)
    moved_cache, attended_t = lax.optimization_barrier((moved_cache, attended_t))
    attended = from_heads(attended_t)
    return (attended, moved_cache)


def solution(mesh):
    return jax.shard_map(
        on_device,
        mesh=mesh,
        in_specs=(
            P("req", "tok", None),
            P("req", "tok", None),
            P("req", "tok", None),
            P("req", None),
            P("req", "tok", None, None, None),
            P("req", "tok", None),
        ),
        out_specs=(P("req", "tok", None), P("req", None, None, None, None, "tok", None)),
        check_vma=False,
    )
```
